256 devices in a mesh: dp: 64 (over y, z_lo, x, core), mp: 4 (over z_hi).
Axes of the slice: x: 4, y: 4, z: 8 (z_hi: 4, z_lo: 2; z = z_hi * 2 + z_lo), core: 2. Of those that a mesh axis runs over, the one named last changes fastest.
Arguments:
- clips: bfloat16 [8192, 768], P('dp', 'mp')
- captions: bfloat16 [8192, 768], P('dp', 'mp')
- video_id: int32 [8192], replicated, may hold values from 0 to 511, never falling along the last dimension, each value on 1 to 128 neighbouring positions
- logit_scale: float32 [], replicated, may hold values from 110 to 160
Outputs:
- d_clips: float32 [8192, 768], P(('dp', 'mp'))
- d_captions: float32 [8192, 768], P(('dp', 'mp'))
The draws below stay inside these ranges and needn't reach their ends.
Inputs may be any that keep to these rules, and one draw needn't show every extreme that they name: `video_id`: video ids never fall along the rows; each video covers 1 to 128 consecutive rows.
All inputs are finite; a program needn't handle non-finite values.
Results may differ from the reference program's by a relative error of at most 0.0095.
Values may be sent and summed in bfloat16 or wider, within the bound.
A program may use at most 64 MiB of HBM per device.

```python
import math
import jax
import jax.numpy as jnp
import numpy as np
from jax import lax

D = 768
ROWS = 128
CLIPS = 8192
VIDEOS = 512


def paired_parts(key):
    shared = jax.random.normal(jax.random.fold_in(key, 101), (CLIPS, D), jnp.float32)
    clip_noise = jax.random.normal(jax.random.fold_in(key, 202), (CLIPS, D), jnp.float32)
    caption_noise = jax.random.normal(jax.random.fold_in(key, 303), (CLIPS, D), jnp.float32)
    aligned = jax.random.bernoulli(jax.random.fold_in(key, 505), 1.0 / 32.0, (CLIPS, 1))
    return (shared, clip_noise, caption_noise, aligned)


def mixed_rows(shared, noise, aligned):
    drawn = 0.42 * shared + noise
    close = shared + 0.05 * noise
    return jnp.where(aligned, close, drawn)


def draw_clips(key, part):
    shared, clip_noise, caption_noise, aligned = paired_parts(key)
    return mixed_rows(shared, clip_noise, aligned).astype(jnp.bfloat16)


def draw_captions(key, part):
    shared, clip_noise, caption_noise, aligned = paired_parts(key)
    return mixed_rows(shared, caption_noise, aligned).astype(jnp.bfloat16)


def split_up(count, total, reach, slope):
    loads = [(1 << 20) // math.isqrt(standing ** slope) + 1 for standing in range(2, count + 1)]
    spare, given = total - reach - (count - 1), [1] * (count - 1)
    while spare > 0:
        free = [i for i in range(count - 1) if given[i] < reach]
        whole, left = sum([loads[i] for i in free]), spare
        for i in free:
            extra = min(reach - given[i], max(1, left * loads[i] // whole), spare)
            given[i] = given[i] + extra
            spare = spare - extra
    return np.array([reach] + given)


def uneven(stream_key, count, total, most, lean):
    if count == 2:
        one = jax.random.randint(stream_key, (), max(1, total - most), min(most, total - 1) + 1)
        return jnp.stack([one, total - one])
    sizes = jnp.asarray(split_up(count, total, most, lean), jnp.int32)
    twos = (count - 1) // 2
    giver, sink = sizes[1:1 + 2 * twos:2], sizes[2:2 + 2 * twos:2]
    margin = jnp.minimum(giver - 1, most - sink)
    passed = jax.random.randint(jax.random.fold_in(stream_key, 1), (twos,), 0, 1 << 20) % (margin + 1)
    sizes = sizes.at[1:1 + 2 * twos:2].set(giver - passed).at[2:2 + 2 * twos:2].set(sink + passed)
    return sizes[jax.random.permutation(jax.random.fold_in(stream_key, 2), count)]


def setup_inputs(seed: int = 0) -> dict:
    splits = jax.random.split(jax.random.key(seed), 5)
    return {
        "clips": draw_clips(jax.random.fold_in(splits[4], 71), 0),
        "captions": draw_captions(jax.random.fold_in(splits[4], 71), 0),
        "video_id": jnp.searchsorted(jnp.cumsum(uneven(splits[2], VIDEOS, CLIPS, ROWS, 2)), jnp.arange(CLIPS), side="right").astype(jnp.int32),
        "logit_scale": jnp.clip(jnp.exp(jax.random.uniform(splits[3], (), jnp.float32, math.log(110.0), math.log(160.0))), 110.0, 160.0),
    }


epsilon = 1e-06
negative_fill = -1e+30

def unit_rows(values):
    widened = values.astype(jnp.float32)
    length = jnp.sqrt(lax.optimization_barrier(jnp.sum(widened * widened, axis=-1)) + epsilon)
    return (widened / length[:, None], length)

def reference(clips, captions, video_id, logit_scale):
    all_rows = clips.shape[0]
    clip_float, clip_length = unit_rows(clips)
    clip_unit = clip_float.astype(jnp.bfloat16)
    cap_float, cap_length = unit_rows(captions)
    cap_unit = cap_float.astype(jnp.bfloat16)
    pooled = jax.ops.segment_sum(clip_unit.astype(jnp.float32), video_id, num_segments=VIDEOS)[video_id]
    pool_length = jnp.sqrt(lax.optimization_barrier(jnp.sum(pooled * pooled, axis=-1)) + epsilon)
    pool_unit = pooled / pool_length[:, None]
    caption_pool = jax.ops.segment_sum(cap_unit.astype(jnp.float32), video_id, num_segments=VIDEOS)[video_id]
    positions = jnp.arange(all_rows, dtype=jnp.int32)
    block_count = all_rows // ROWS

    def block_scores(query_units, other_units, block_index):
        first_row = (block_index * ROWS).astype(jnp.int32)
        query_rows = lax.dynamic_slice_in_dim(query_units, first_row, ROWS, 0)
        row_videos = lax.dynamic_slice_in_dim(video_id, first_row, ROWS, 0)
        row_positions = first_row + jnp.arange(ROWS, dtype=jnp.int32)
        scores = logit_scale * jnp.dot(query_rows, other_units.T, preferred_element_type=jnp.float32)
        allowed = (row_videos[:, None] != video_id[None, :]) | (row_positions[:, None] == positions[None, :])
        return (scores, allowed, query_rows, first_row)

    def log_totals(query_units, other_units):

        def one_block(block_index):
            scores, allowed, query_rows, first_row = block_scores(query_units, other_units, block_index)
            top_score = lax.optimization_barrier(jnp.max(jnp.where(allowed, scores, negative_fill), axis=1))
            totals = lax.optimization_barrier(jnp.sum(jnp.where(allowed, jnp.exp(scores - top_score[:, None]), 0.0), axis=1))
            return top_score + jnp.log(totals)
        return lax.map(one_block, jnp.arange(block_count, dtype=jnp.int32)).reshape(all_rows)
    row_lse = log_totals(clip_unit, cap_unit)
    col_lse = log_totals(cap_unit, clip_unit)

    def backward_block(cap_acc, block_index):
        scores, allowed, query_rows, first_row = block_scores(clip_unit, cap_unit, block_index)
        row_part = lax.dynamic_slice_in_dim(row_lse, first_row, ROWS, 0)
        weights = 0.5 * (jnp.exp(scores - row_part[:, None]) + jnp.exp(scores - col_lse[None, :]))
        weights = jnp.where(allowed, weights, 0.0).astype(jnp.bfloat16)
        clip_part = jnp.dot(weights, cap_unit, preferred_element_type=jnp.float32)
        cap_acc = cap_acc + jnp.dot(weights.T, query_rows, preferred_element_type=jnp.float32)
        return (cap_acc, clip_part)
    cap_acc, clip_parts = lax.scan(backward_block, jnp.zeros((all_rows, clips.shape[1]), jnp.float32), jnp.arange(block_count, dtype=jnp.int32))
    clip_acc = clip_parts.reshape(all_rows, clips.shape[1])
    projected = caption_pool - pool_unit * lax.optimization_barrier(jnp.sum(pool_unit * caption_pool, axis=-1, keepdims=True))
    clip_grad_unit = logit_scale * clip_acc - 0.5 * logit_scale * cap_unit.astype(jnp.float32) - 0.5 * logit_scale * projected / pool_length[:, None]
    cap_grad_unit = logit_scale * cap_acc - 0.5 * logit_scale * clip_unit.astype(jnp.float32) - 0.5 * logit_scale * pool_unit
    d_clips = (clip_grad_unit - clip_float * lax.optimization_barrier(jnp.sum(clip_float * clip_grad_unit, axis=-1, keepdims=True))) / clip_length[:, None]
    d_captions = (cap_grad_unit - cap_float * lax.optimization_barrier(jnp.sum(cap_float * cap_grad_unit, axis=-1, keepdims=True))) / cap_length[:, None]
    return (d_clips, d_captions)
```

```python
import jax
import jax.numpy as jnp
from jax import lax
from jax.experimental import pallas as pl
from jax.experimental.pallas import tpu as pltpu
from jax.sharding import PartitionSpec as P

EPSILON = 1e-06
NEGATIVE_FILL = -1e30
F32 = jnp.float32
BF16 = jnp.bfloat16
MESH = pl.DeviceIdType.MESH


def chip(x, y, z, core):
    return ((y * 2 + lax.rem(z, 2)) * 8 + x * 2 + core, lax.div(z, 2))


def kernel(
    scale_ref, vid_ref, clips_ref, caps_ref,
    dclip_ref, dcap_ref,
    ca, ta, hclip, hcap, hlen,
    cl, ct, vi, vj,
    pu, plen, eo, ei,
    sc, same, wt, pj,
    rst, rsib, rcomb, rz, cst, cx, ccomb, cy,
    g, sb, hb, hown, rzs,
    g2, pc, qy, qx, r0, r1, r0b, r1b, fx, fy,
    a2a_s, a2a_r, z_s, z_r, s_s, s_r, p_s, p_r, e_s, e_r,
    t_s, t_r, u_s, u_r, w_s, w_r, v_s, v_r,
):
    dp = lax.axis_index("dp")
    zh = lax.axis_index("mp")
    core = lax.rem(dp, 2)
    x = lax.rem(lax.div(dp, 2), 4)
    zl = lax.rem(lax.div(dp, 8), 2)
    y = lax.div(dp, 16)
    z = zh * 2 + zl
    mine = zl * 8 + core * 4 + zh
    sibling = chip(x, y, z, 1 - core)
    at_z = lambda d: chip(x, y, lax.rem(z + d, 8), core)
    at_x = lambda d: chip(lax.rem(x + d, 4), y, z, core)
    at_y = lambda d: chip(x, lax.rem(y + d, 4), z, core)

    def copy(src, dst, send, recv, device):
        c = pltpu.make_async_remote_copy(
            src_ref=src, dst_ref=dst, send_sem=send, recv_sem=recv,
            device_id=device, device_id_type=MESH,
        )
        c.start()
        return c

    runs = [y * 8 + x, y * 8 + 4 + x]

    def owner(q):
        return chip(lax.rem(q, 4), lax.div(q, 8), z, core), lax.rem(lax.div(q, 4), 2)

    after = [owner(lax.rem(q + 1, 32)) for q in runs]
    before = [owner(lax.rem(q + 31, 32)) for q in runs]

    barrier = pltpu.get_barrier_semaphore()
    partners = [sibling] + [at_z(d) for d in range(1, 8)]
    partners += [at_x(d) for d in range(1, 4)] + [at_y(d) for d in range(1, 4)]
    partners += [device for device, _ in after + before]
    for device in partners:
        pl.semaphore_signal(barrier, inc=1, device_id=device, device_id_type=MESH)

    sub = lax.broadcasted_iota(jnp.int32, (128, 128), 0)
    lane = lax.broadcasted_iota(jnp.int32, (128, 128), 1)
    eye = sub == lane

    def to_col(row):
        return jnp.sum(jnp.where(eye, row, 0.0), axis=1, keepdims=True)

    def to_row(col):
        return jnp.sum(jnp.where(eye, col, 0.0), axis=0, keepdims=True)

    def block_of(b):
        return (y * 2 + lax.div(b, 2)) * 8 + x * 2 + lax.rem(b, 2)

    for b in range(4):
        vi[b] = to_col(vid_ref[pl.ds(block_of(b), 1), :])
    segment = lax.div(lax.broadcasted_iota(jnp.int32, (1, 128), 1), 16)
    for h in range(2):
        for grp in range(2):
            out = jnp.zeros((1, 128), F32)
            for s in range(8):
                a, b = grp * 2 + s // 4, s % 4
                ys, xs = (a, b) if h == 0 else (b, a)
                v = vid_ref[pl.ds((ys * 2 + zl) * 8 + xs * 2 + core, 1), :]
                shift = lax.rem(s * 16 + 256 - zh * 32 - h * 16, 128)
                out = jnp.where(segment == s, pltpu.roll(v, shift, 1), out)
            vj[:, (h * 2 + grp) * 128:(h * 2 + grp + 1) * 128] = out

    pl.semaphore_wait(barrier, len(partners))

    pending = []
    for d in range(1, 4):
        to = lax.rem(zh + d, 4)
        rows = pl.ds(pl.multiple_of(to * 32, 32), 32)
        for i, (src, dst) in enumerate(((caps_ref, ta), (clips_ref, ca))):
            pending.append(
                copy(src.at[rows, :], dst.at[zh], a2a_s.at[i, d], a2a_r.at[i, d], (dp, to))
            )
    own = pl.ds(pl.multiple_of(zh * 32, 32), 32)
    ca[zh] = clips_ref[own, :]
    ta[zh] = caps_ref[own, :]

    def unit(parts, held, i):
        full = jnp.concatenate([parts[k].astype(F32) for k in range(4)], axis=1)
        length = jnp.sqrt(jnp.sum(full * full, axis=1, keepdims=True) + EPSILON)
        value = full / length
        held[...] = value
        hlen[i] = length
        return value.astype(BF16)

    for c in pending[0::2]:
        c.wait()
    u = unit(ta, hcap, 1)
    ct[0, y, x] = u[0:16]
    ct[1, x, y] = u[16:32]
    stage_a = []
    for d in (2, 1, 3):
        src = ct.at[0, y, x]
        stage_a.append(copy(src, src, p_s.at[0, d], p_r.at[0, d], at_x(d)))
        src = ct.at[1, x, y]
        stage_a.append(copy(src, src, p_s.at[1, d], p_r.at[1, d], at_y(d)))
    for c in pending[1::2]:
        c.wait()
    cl[mine] = unit(ca, hclip, 0)
    z_copies = []
    src = cl.at[mine]
    sib_copies = [copy(src, src, s_s.at[0], s_r.at[0], sibling)]
    for d in (4, 3, 5, 2, 6, 1, 7):
        z_copies.append((d, copy(src, src, z_s.at[d], z_r.at[d], at_z(d))))
    for c in stage_a:
        c.wait()
    stage_b = []
    for d in (2, 1, 3):
        src = ct.at[0, y]
        stage_b.append(copy(src, src, p_s.at[2, d], p_r.at[2, d], at_y(d)))
        src = ct.at[1, x]
        stage_b.append(copy(src, src, p_s.at[3, d], p_r.at[3, d], at_x(d)))
    for d, c in sorted(z_copies, key=lambda t: min(t[0], 8 - t[0])):
        c.wait()
        zs = lax.rem(z + 8 - d, 8)
        src = cl.at[lax.rem(zs, 2) * 8 + core * 4 + lax.div(zs, 2)]
        sib_copies.append(copy(src, src, s_s.at[d], s_r.at[d], sibling))
    for c in sib_copies:
        c.wait()

    edge_copies = []
    for r in range(2):
        units = cl[8 * r:8 * r + 8].reshape(256, 768)
        ids = jnp.concatenate([vid_ref[pl.ds(block_of(2 * r + i), 1), :] for i in range(2)], axis=1)
        col = jnp.concatenate([vi[2 * r], vi[2 * r + 1]], axis=0)
        alike = jnp.where(col == ids, 1.0, 0.0).astype(BF16)
        local = jnp.dot(alike, units, preferred_element_type=F32)
        pu[2 * r] = local[0:128]
        pu[2 * r + 1] = local[128:256]
        eo[2 * r] = local[0:1]
        eo[2 * r + 1] = local[255:256]
        device, slot = before[r]
        edge_copies.append(
            copy(eo.at[2 * r], ei.at[slot * 2 + 1], e_s.at[2 * r], e_r.at[slot * 2 + 1], device)
        )
        device, slot = after[r]
        edge_copies.append(
            copy(eo.at[2 * r + 1], ei.at[slot * 2], e_s.at[2 * r + 1], e_r.at[slot * 2], device)
        )
    for c in stage_b:
        c.wait()

    scale = scale_ref[0]
    captions = ct[...].reshape(512, 768)
    sc[...] = lax.dot_general(
        cl[...].reshape(512, 768), captions, (((1,), (1,)), ((), ())), preferred_element_type=F32
    ).reshape(4, 128, 512)
    column = lax.broadcasted_iota(jnp.int32, (1, 512), 1)
    half = lax.div(column, 256)
    first = lax.rem(lax.div(column, 64), 4)
    second = lax.rem(lax.div(column, 16), 4)
    ypos = jnp.where(half == 0, first, second)
    xpos = jnp.where(half == 0, second, first)
    col_pos = ((ypos * 2 + zl) * 8 + xpos * 2 + core) * 128 + zh * 32 + half * 16
    col_pos = col_pos + lax.rem(column, 16)

    def pass_one(b, col_max):
        row_pos = block_of(b) * 128 + lax.broadcasted_iota(jnp.int32, (128, 1), 0)
        alike = vi[b] == vj[...]
        allowed = jnp.logical_not(alike) | (row_pos == col_pos)
        s = jnp.where(allowed, scale * sc[b], NEGATIVE_FILL)
        sc[b] = s
        same[b] = jnp.where(alike, 1.0, 0.0).astype(BF16)
        top = jnp.max(s, axis=1, keepdims=True)
        total = jnp.sum(jnp.exp(s - top), axis=1, keepdims=True)
        rst[pl.ds(b, 1), :] = to_row(top)
        rst[pl.ds(4 + b, 1), :] = to_row(total)
        return jnp.maximum(col_max, jnp.max(s, axis=0, keepdims=True))

    col_max = lax.fori_loop(0, 4, pass_one, jnp.full((1, 512), NEGATIVE_FILL, F32))
    stats = [copy(rst, rsib, t_s.at[0], t_r.at[0], sibling)]

    def pass_two(b, total):
        return total + jnp.sum(jnp.exp(sc[b] - col_max), axis=0, keepdims=True)

    col_sum = lax.fori_loop(0, 4, pass_two, jnp.zeros((1, 512), F32))
    for b in range(4):
        cst[b:b + 1, :] = col_max[:, b * 128:(b + 1) * 128]
        cst[4 + b:5 + b, :] = col_sum[:, b * 128:(b + 1) * 128]
    for d in (2, 1, 3):
        stats.append(copy(cst, cx.at[d], t_s.at[d], t_r.at[d], at_x(d)))

    edge_ids = []
    for r in range(2):
        q = runs[r]
        left = vid_ref[pl.ds(jnp.maximum(2 * q - 1, 0), 1), :][:, 127:128]
        right = vid_ref[pl.ds(jnp.minimum(2 * q + 2, 63), 1), :][:, 0:1]
        edge_ids.append((left, right, jnp.where(q > 0, 1.0, 0.0), jnp.where(q < 31, 1.0, 0.0)))
    for c in edge_copies:
        c.wait()
    for b in range(4):
        r = b // 2
        left, right, has_left, has_right = edge_ids[r]
        from_left = jnp.where(vi[b] == left, has_left, 0.0)
        from_right = jnp.where(vi[b] == right, has_right, 0.0)
        pooled = pu[b] + from_left * ei[2 * r] + from_right * ei[2 * r + 1]
        length = jnp.sqrt(jnp.sum(pooled * pooled, axis=1, keepdims=True) + EPSILON)
        plen[b] = length
        pu[b] = pooled / length

    def joined(first, others):
        top, total = first
        for m, s in others:
            new = jnp.maximum(top, m)
            total = total * jnp.exp(top - new) + s * jnp.exp(m - new)
            top = new
        return top, total

    for c in stats:
        c.wait()
    top, total = joined((rst[0:4], rst[4:8]), [(rsib[0:4], rsib[4:8])])
    rcomb[0:4] = top
    rcomb[4:8] = total
    stats = [copy(rcomb, rz.at[d], u_s.at[0, d], u_r.at[0, d], at_z(d)) for d in (4, 3, 5, 2, 6, 1, 7)]
    row_pair = (top, total)
    top, total = joined((cst[0:4], cst[4:8]), [(cx[d, 0:4], cx[d, 4:8]) for d in range(1, 4)])
    ccomb[0:4] = top
    ccomb[4:8] = total
    stats += [copy(ccomb, cy.at[d], u_s.at[1, d], u_r.at[1, d], at_y(d)) for d in (2, 1, 3)]
    col_pair = (top, total)

    def projected(b, carry):
        acc = jnp.dot(same[b], ct[...].reshape(512, 768), preferred_element_type=F32)
        pool = pu[b]
        acc = acc - pool * jnp.sum(pool * acc, axis=1, keepdims=True)
        pj[b] = acc * (0.5 / plen[b])
        return carry

    lax.fori_loop(0, 4, projected, 0)

    for c in stats:
        c.wait()
    top, total = joined(row_pair, [(rz[d, 0:4], rz[d, 4:8]) for d in range(1, 8)])
    row_lse = top + jnp.log(total)
    top, total = joined(col_pair, [(cy[d, 0:4], cy[d, 4:8]) for d in range(1, 4)])
    col_lse = top + jnp.log(total)
    col_lse = jnp.concatenate([col_lse[b:b + 1] for b in range(4)], axis=1)
    rst[0:4] = row_lse

    def weigh(b, carry):
        rows = to_col(rst[pl.ds(b, 1), :])
        s = sc[b]
        w = 0.5 * (jnp.exp(s - rows) + jnp.exp(s - col_lse))
        w = w.astype(BF16)
        wt[b] = w
        part = jnp.dot(w, ct[...].reshape(512, 768), preferred_element_type=F32) - pj[b]
        pj[b] = part
        g[pl.ds(pl.multiple_of(4 * b, 4), 4)] = part.astype(BF16).reshape(4, 32, 768)
        return carry

    lax.fori_loop(0, 4, weigh, 0)
    sib_copies = []
    for r in range(2):
        src = g.at[pl.ds(pl.multiple_of(8 * r + 4 * (1 - core), 4), 4)]
        sib_copies.append(copy(src, sb.at[r], w_s.at[0, r], w_r.at[0, r], sibling))

    part = lax.dot_general(
        wt[...].reshape(512, 512), cl[...].reshape(512, 768), (((0,), (0,)), ((), ())),
        preferred_element_type=F32,
    ).reshape(2, 4, 4, 16, 768)
    pc[...] = part
    g2[...] = part.astype(BF16)
    stage_a = []
    for d in (2, 1, 3):
        src = g2.at[0, lax.rem(y + d, 4)]
        stage_a.append(copy(src, qy.at[d], v_s.at[0, d], v_r.at[0, d], at_y(d)))
        src = g2.at[1, lax.rem(x + d, 4)]
        stage_a.append(copy(src, qx.at[d], v_s.at[1, d], v_r.at[1, d], at_x(d)))

    for c in sib_copies:
        c.wait()
    for r in range(2):
        both = pj[2 * r + core].reshape(4, 32, 768) + sb[r].astype(F32)
        hown[r] = both
        hb[r] = both.astype(BF16)
    z_copies = []
    for d in (4, 3, 5, 2, 6, 1, 7):
        to = lax.rem(z + d, 8)
        src = hb.at[lax.rem(to, 2), lax.div(to, 2)]
        z_copies.append(copy(src, rzs.at[d], w_s.at[1, d], w_r.at[1, d], at_z(d)))

    for c in stage_a:
        c.wait()
    total = pc[0, y] + qy[1].astype(F32) + qy[2].astype(F32) + qy[3].astype(F32)
    r0[...] = total
    r0b[...] = total.astype(BF16)
    total = pc[1, x] + qx[1].astype(F32) + qx[2].astype(F32) + qx[3].astype(F32)
    r1[...] = total
    r1b[...] = total.astype(BF16)
    stage_b = []
    for d in (2, 1, 3):
        src = r0b.at[lax.rem(x + d, 4)]
        stage_b.append(copy(src, fx.at[d], v_s.at[2, d], v_r.at[2, d], at_x(d)))
        src = r1b.at[lax.rem(y + d, 4)]
        stage_b.append(copy(src, fy.at[d], v_s.at[3, d], v_r.at[3, d], at_y(d)))
    for c in stage_b:
        c.wait()

    low = r0[x] + fx[1].astype(F32) + fx[2].astype(F32) + fx[3].astype(F32)
    high = r1[y] + fy[1].astype(F32) + fy[2].astype(F32) + fy[3].astype(F32)
    acc = jnp.concatenate([low, high], axis=0)
    held = hcap[...]
    clip_held = hclip[...]
    clip_unit = clip_held.astype(BF16).astype(F32)
    cap_unit = held.astype(BF16).astype(F32)
    pool_unit = pu[zl * 2 + core, pl.ds(pl.multiple_of(zh * 32, 32), 32), :]
    grad = scale * acc - 0.5 * scale * clip_unit - 0.5 * scale * pool_unit
    dcap_ref[...] = (grad - held * jnp.sum(held * grad, axis=1, keepdims=True)) / hlen[1]

    for c in z_copies:
        c.wait()
    acc = hown[zl, zh]
    for d in range(1, 8):
        acc = acc + rzs[d].astype(F32)
    grad = scale * acc - 0.5 * scale * cap_unit
    dclip_ref[...] = (
        grad - clip_held * jnp.sum(clip_held * grad, axis=1, keepdims=True)
    ) / hlen[0]


def body(clips, captions, video_id, logit_scale):
    vmem = pl.BlockSpec(memory_space=pltpu.VMEM)
    dma = lambda *shape: pltpu.SemaphoreType.DMA(shape)
    out = jax.ShapeDtypeStruct((32, 768), F32)
    V = pltpu.VMEM
    ids = video_id.reshape(64, 128).astype(F32)
    return pl.pallas_call(
        kernel,
        out_shape=(out, out),
        in_specs=[pl.BlockSpec(memory_space=pltpu.SMEM), vmem, vmem, vmem],
        out_specs=(vmem, vmem),
        scratch_shapes=[
            V((4, 32, 192), BF16), V((4, 32, 192), BF16),
            V((32, 768), F32), V((32, 768), F32), V((2, 32, 1), F32),
            V((16, 32, 768), BF16), V((2, 4, 4, 16, 768), BF16),
            V((4, 128, 1), F32), V((1, 512), F32),
            V((4, 128, 768), F32), V((4, 128, 1), F32), V((4, 1, 768), F32), V((4, 1, 768), F32),
            V((4, 128, 512), F32), V((4, 128, 512), BF16), V((4, 128, 512), BF16),
            V((4, 128, 768), F32),
            V((8, 128), F32), V((8, 128), F32), V((8, 128), F32), V((8, 8, 128), F32),
            V((8, 128), F32), V((4, 8, 128), F32), V((8, 128), F32), V((4, 8, 128), F32),
            V((16, 32, 768), BF16), V((2, 4, 32, 768), BF16), V((2, 4, 32, 768), BF16),
            V((2, 4, 32, 768), F32), V((8, 32, 768), BF16),
            V((2, 4, 4, 16, 768), BF16), V((2, 4, 4, 16, 768), F32),
            V((4, 4, 16, 768), BF16), V((4, 4, 16, 768), BF16),
            V((4, 16, 768), F32), V((4, 16, 768), F32),
            V((4, 16, 768), BF16), V((4, 16, 768), BF16),
            V((4, 16, 768), BF16), V((4, 16, 768), BF16),
            dma(2, 4), dma(2, 4), dma(8), dma(8), dma(8), dma(8), dma(4, 4), dma(4, 4),
            dma(4), dma(4), dma(4), dma(4), dma(2, 8), dma(2, 8), dma(2, 8), dma(2, 8),
            dma(4, 4), dma(4, 4),
        ],
        compiler_params=pltpu.CompilerParams(
            collective_id=0, has_side_effects=True, vmem_limit_bytes=48 * 1024 * 1024
        ),
        name="contrastive",
    )(logit_scale.reshape(1), ids, clips, captions)


def solution(mesh):
    in_specs = (P("dp", "mp"), P("dp", "mp"), P(), P())
    out_specs = (P(("dp", "mp"), None), P(("dp", "mp"), None))
    return jax.shard_map(body, mesh=mesh, in_specs=in_specs, out_specs=out_specs, check_vma=False)
```

```python
import jax
import jax.numpy as jnp
from jax import lax
from jax.experimental import pallas as pl
from jax.experimental.pallas import tpu as pltpu
from jax.sharding import PartitionSpec as P

EPSILON = 1e-06
NEGATIVE_FILL = -1e30
F32 = jnp.float32
BF16 = jnp.bfloat16
MESH = pl.DeviceIdType.MESH


def chip(x, y, z, core):
    return ((y * 2 + lax.rem(z, 2)) * 8 + x * 2 + core, lax.div(z, 2))


def kernel(
    scale_ref, vid_ref, clips_ref, caps_ref,
    dclip_ref, dcap_ref,
    raw, vid, pkt, ta, cr, hcap, hclip, hlen,
    clt, ct, vic, vjr, vir, vjc,
    pu, plen, eo, ei,
    ej, ek, ejt, ekt, pj,
    rst, rz, cst, cz,
    g, sb, hb, hown, rzs,
    pc, g2, got,
    l_s, a2a_s, a2a_r, z_s, z_r, s_s, s_r, p_s, p_r, e_s, e_r,
    t_s, t_r, w_s, w_r, v_s, v_r,
):
    dp = lax.axis_index("dp")
    zh = lax.axis_index("mp")
    core = lax.rem(dp, 2)
    x = lax.rem(lax.div(dp, 2), 4)
    zl = lax.rem(lax.div(dp, 8), 2)
    y = lax.div(dp, 16)
    z = zh * 2 + zl
    home = zl * 2 + core
    sibling = chip(x, y, z, 1 - core)
    at_z = lambda d: chip(x, y, lax.rem(z + d, 8), core)
    at_xy = lambda i, j: chip(lax.rem(x + i, 4), lax.rem(y + j, 4), z, core)
    others_z = (4, 3, 5, 2, 6, 1, 7)
    others_xy = sorted(
        [(i, j) for i in range(4) for j in range(4) if i or j],
        key=lambda t: -(min(t[0], 4 - t[0]) + min(t[1], 4 - t[1])),
    )

    def copy(src, dst, send, recv, device):
        c = pltpu.make_async_remote_copy(
            src_ref=src, dst_ref=dst, send_sem=send, recv_sem=recv,
            device_id=device, device_id_type=MESH,
        )
        c.start()
        return c

    runs = [y * 8 + x, y * 8 + 4 + x]

    def owner(q):
        return chip(lax.rem(q, 4), lax.div(q, 8), z, core), lax.rem(lax.div(q, 4), 2)

    after = [owner(lax.rem(q + 1, 32)) for q in runs]
    before = [owner(lax.rem(q + 31, 32)) for q in runs]

    barrier = pltpu.get_barrier_semaphore()
    partners = [at_z(d) for d in others_z]
    partners += [chip(x, y, lax.rem(z + d, 8), 1 - core) for d in others_z]
    partners += [at_xy(i, j) for i, j in others_xy] + [sibling]
    for device in partners:
        pl.semaphore_signal(barrier, inc=1, device_id=device, device_id_type=MESH)
    loads = [
        pltpu.make_async_copy(src, dst, l_s.at[i])
        for i, (src, dst) in enumerate(((caps_ref, raw.at[1]), (clips_ref, raw.at[0]), (vid_ref, vid)))
    ]
    for c in loads:
        c.start()

    loads[0].wait()
    block = raw[1].astype(F32).T
    for k in range(4):
        pkt[k, 0:32] = block[32 * k:32 * k + 32, 0:128].astype(BF16)
        tail = block[32 * k:32 * k + 32, 128:192]
        pkt[k, 32:48] = jnp.concatenate([tail[0:16], tail[16:32]], axis=1).astype(BF16)
    ta[zh] = pkt[zh]
    loads[1].wait()
    slot = lambda at, c: lax.rem(at, 2) * 8 + c * 4 + lax.div(at, 2)
    mine = slot(z, core)
    cr[mine] = raw[0]

    loads[2].wait()
    sub = lax.broadcasted_iota(jnp.int32, (128, 128), 0)
    lane = lax.broadcasted_iota(jnp.int32, (128, 128), 1)
    eye = sub == lane

    def to_col(row):
        return jnp.sum(jnp.where(eye, row, 0.0), axis=1, keepdims=True)

    def to_row(col):
        return jnp.sum(jnp.where(eye, col, 0.0), axis=0, keepdims=True)

    def block_of(b):
        return (y * 2 + lax.div(b, 2)) * 8 + x * 2 + lax.rem(b, 2)

    def ids_of(row):
        return vid[pl.ds(row, 1), :].astype(F32)

    for b in range(4):
        ids = ids_of(block_of(b))
        vir[:, 128 * b:128 * b + 128] = ids
        vic[b] = to_col(ids)
    segment = lax.div(lax.broadcasted_iota(jnp.int32, (1, 128), 1), 32)
    for b in range(4):
        out = jnp.zeros((1, 128), F32)
        for i in range(4):
            v = ids_of((b * 2 + zl) * 8 + i * 2 + core)
            out = jnp.where(segment == i, pltpu.roll(v, lax.rem((i + 4 - zh) * 32, 128), 1), out)
        vjr[:, 128 * b:128 * b + 128] = out
        vjc[b] = to_col(out)

    pl.semaphore_wait(barrier, len(partners))

    pending = []
    for d in (2, 1, 3):
        to = lax.rem(zh + d, 4)
        pending.append(copy(pkt.at[to], ta.at[zh], a2a_s.at[d], a2a_r.at[d], (dp, to)))
    own = raw.at[0]
    sib_copies = [copy(own, cr.at[mine], s_s.at[0], s_r.at[0], sibling)]
    z_copies = [
        (d, copy(own, cr.at[mine], z_s.at[d], z_r.at[d], at_z(d))) for d in others_z
    ]

    def unpacked(parts):
        low = lax.broadcasted_iota(jnp.int32, (16, 128), 1) < 64
        tiles = [p[0:32].astype(F32) for p in parts]
        tails = [p[32:48].astype(F32) for p in parts]
        for i in (0, 2):
            left, right = tails[i], tails[i + 1]
            upper = jnp.where(low, left, pltpu.roll(right, 64, 1))
            lower = jnp.where(low, pltpu.roll(left, 64, 1), right)
            tiles.append(jnp.concatenate([upper, lower], axis=0))
        return jnp.concatenate(tiles, axis=1)

    def lengths(full):
        return jnp.sqrt(jnp.sum(full * full, axis=1, keepdims=True) + EPSILON)

    for c in pending:
        c.wait()
    full = unpacked([ta[k] for k in range(4)])
    length = lengths(full)
    full = full / length
    hcap[...] = full
    hlen[1] = length
    u = full.astype(BF16)
    at = y * 4 + x
    ct[at] = u
    plane = []
    for i, j in others_xy:
        ref = ct.at[at]
        plane.append(copy(ref, ref, p_s.at[i, j], p_r.at[i, j], at_xy(i, j)))
    for d, c in z_copies:
        c.wait()
        ref = cr.at[slot(lax.rem(z + 8 - d, 8), core)]
        sib_copies.append(copy(ref, ref, s_s.at[d], s_r.at[d], sibling))
    for c in sib_copies:
        c.wait()

    def normalise(b, carry):
        parts = [cr[4 * b + k].astype(F32) for k in range(4)]
        total = sum(jnp.sum(p * p, axis=0, keepdims=True) for p in parts)
        inverse = 1.0 / jnp.sqrt(total + EPSILON)
        columns = pl.ds(pl.multiple_of(128 * b, 128), 128)
        for k, p in enumerate(parts):
            p = (p * inverse).astype(BF16)
            clt[128 * k:128 * k + 128, columns] = p[0:128]
            clt[512 + 64 * k:576 + 64 * k, columns] = p[128:192]
        return carry

    lax.fori_loop(0, 4, normalise, 0)
    for c in plane:
        c.wait()

    scale = scale_ref[0]
    ej[...] = jnp.dot(
        ct[...].reshape(512, 768), clt[...], preferred_element_type=F32
    ).reshape(4, 128, 512)
    column = lax.broadcasted_iota(jnp.int32, (1, 512), 1)
    clip_pos = (y * 2 + lax.div(column, 256)) * 1024 + x * 256 + lax.rem(column, 256)

    def pass_one(b, top):
        j = b * 128 + lax.broadcasted_iota(jnp.int32, (128, 1), 0)
        cap_pos = ((b * 2 + zl) * 8 + lax.rem(lax.div(j, 32), 4) * 2 + core) * 128
        cap_pos = cap_pos + zh * 32 + lax.rem(j, 32)
        alike = vjc[b] == vir[...]
        allowed = jnp.logical_not(alike) | (cap_pos == clip_pos)
        s = jnp.where(allowed, scale * ej[b], NEGATIVE_FILL)
        ej[b] = s
        return jnp.maximum(top, jnp.max(s, axis=0, keepdims=True))

    clip_top = lax.fori_loop(0, 4, pass_one, jnp.full((1, 512), NEGATIVE_FILL, F32))

    def pass_two(b, total):
        e = jnp.exp(ej[b] - clip_top)
        ek[b] = e
        return total + jnp.sum(e, axis=0, keepdims=True)

    clip_sum = lax.fori_loop(0, 4, pass_two, jnp.zeros((1, 512), F32))
    for b in range(4):
        rst[b:b + 1, :] = clip_top[:, b * 128:(b + 1) * 128]
        rst[4 + b:5 + b, :] = clip_sum[:, b * 128:(b + 1) * 128]
    stats = []
    for d in others_z + (0,):
        for i in range(2):
            if d or i:
                n = i * 8 + d
                device = chip(x, y, lax.rem(z + d, 8), core if i == 0 else 1 - core)
                stats.append(copy(rst, rz.at[n], t_s.at[0, n], t_r.at[0, n], device))

    def pass_three(b, carry):
        s = ej[b]
        top = jnp.max(s, axis=1, keepdims=True)
        e = jnp.exp(s - top)
        ej[b] = e
        cst[pl.ds(b, 1), :] = to_row(top)
        cst[pl.ds(4 + b, 1), :] = to_row(jnp.sum(e, axis=1, keepdims=True))
        return carry

    lax.fori_loop(0, 4, pass_three, 0)
    for i, j in others_xy:
        n = i * 4 + j
        stats.append(copy(cst, cz.at[n], t_s.at[1, n], t_r.at[1, n], at_xy(i, j)))
    rz[0] = rst[...]
    cz[0] = cst[...]

    def joined(ref):
        tops = ref[:, 0:4]
        top = jnp.max(tops, axis=0)
        return top + jnp.log(jnp.sum(ref[:, 4:8] * jnp.exp(tops - top), axis=0))

    edge_copies = []
    for r in range(2):
        ids = vir[:, 256 * r:256 * r + 256]
        col = jnp.concatenate([vic[2 * r], vic[2 * r + 1]], axis=0)
        alike = jnp.where(col == ids, 1.0, 0.0).astype(BF16)
        local = lax.dot_general(
            alike, clt[:, 256 * r:256 * r + 256], (((1,), (1,)), ((), ())),
            preferred_element_type=F32,
        )
        pu[2 * r] = local[0:128]
        pu[2 * r + 1] = local[128:256]
        eo[2 * r] = local[0:1]
        eo[2 * r + 1] = local[255:256]
        device, side = before[r]
        edge_copies.append(
            copy(eo.at[2 * r], ei.at[side * 2 + 1], e_s.at[2 * r], e_r.at[side * 2 + 1], device)
        )
        device, side = after[r]
        edge_copies.append(
            copy(eo.at[2 * r + 1], ei.at[side * 2], e_s.at[2 * r + 1], e_r.at[side * 2], device)
        )

    for b in range(4):
        ejt[:, b * 128:(b + 1) * 128] = ej[b].T
        ekt[:, b * 128:(b + 1) * 128] = ek[b].T
    parts = [cr[4 * home + k].astype(F32) for k in range(4)]
    full = jnp.concatenate([p[0:128] for p in parts] + [p[128:192] for p in parts], axis=0)
    pj[0] = full.T
    rows = pl.ds(pl.multiple_of(zh * 32, 32), 32)
    full = pj[0, rows, :]
    length = lengths(full)
    hclip[...] = full / length
    hlen[0] = length
    for c in edge_copies:
        c.wait()
    for b in range(4):
        r = b // 2
        q = runs[r]
        left = ids_of(jnp.maximum(2 * q - 1, 0))[:, 127:128]
        right = ids_of(jnp.minimum(2 * q + 2, 63))[:, 0:1]
        from_left = jnp.where(vic[b] == left, jnp.where(q > 0, 1.0, 0.0), 0.0)
        from_right = jnp.where(vic[b] == right, jnp.where(q < 31, 1.0, 0.0), 0.0)
        pooled = pu[b] + from_left * ei[2 * r] + from_right * ei[2 * r + 1]
        length = lengths(pooled)
        plen[b] = length
        pu[b] = pooled * (1.0 / length)

    def projected(b, carry):
        alike = jnp.where(vic[b] == vjr[...], 1.0, 0.0).astype(BF16)
        acc = jnp.dot(alike, ct[...].reshape(512, 768), preferred_element_type=F32)
        pool = pu[b]
        acc = acc - pool * jnp.sum(pool * acc, axis=1, keepdims=True)
        pj[b] = acc * (0.5 / plen[b])
        return carry

    lax.fori_loop(0, 4, projected, 0)

    for c in stats:
        c.wait()
    clip_fac = 0.5 * jnp.exp(rst[0:4] - joined(rz))
    cap_fac = 0.5 * jnp.exp(cst[0:4] - joined(cz))
    clip_line = jnp.concatenate([clip_fac[b:b + 1] for b in range(4)], axis=1)
    cap_line = jnp.concatenate([cap_fac[b:b + 1] for b in range(4)], axis=1)
    rst[0:4] = clip_fac
    cst[0:4] = cap_fac

    def weigh(c):
        blocks = [c, 2 + c]
        w = []
        for b in blocks:
            rows = pl.ds(pl.multiple_of(128 * b, 128), 128)
            w.append(
                (ekt[rows, :] * to_col(rst[pl.ds(b, 1), :]) + ejt[rows, :] * cap_line).astype(BF16)
            )
        part = jnp.dot(
            jnp.concatenate(w, axis=0), ct[...].reshape(512, 768), preferred_element_type=F32
        )
        return [part[128 * i:128 * i + 128] - pj[b] for i, b in enumerate(blocks)]

    sib_copies = []
    for r, part in enumerate(weigh(1 - core)):
        g[r] = part.astype(BF16).reshape(4, 32, 768)
        sib_copies.append(copy(g.at[r], sb.at[r], w_s.at[0, r], w_r.at[0, r], sibling))
    for r, part in enumerate(weigh(core)):
        hown[r] = part.reshape(4, 32, 768)


    back = []

    def caption_part(offsets):
        blocks = [lax.rem(y + j, 4) for j in offsets]
        w = [
            (ek[b] * clip_line + ej[b] * to_col(cst[pl.ds(b, 1), :])).astype(BF16) for b in blocks
        ]
        part = lax.dot_general(
            jnp.concatenate(w, axis=0), clt[...], (((1,), (1,)), ((), ())),
            preferred_element_type=F32,
        ).reshape(2, 4, 32, 768)
        for n, j in enumerate(offsets):
            g2[j] = part[n].astype(BF16)
            if j == 0:
                pc[...] = part[n]
            for i in (2, 1, 3, 0):
                if i or j:
                    src = g2.at[j, lax.rem(x + i, 4)]
                    back.append(
                        copy(src, got.at[i * 4 + j], v_s.at[i, j], v_r.at[i, j], at_xy(i, j))
                    )

    caption_part((2, 1))
    z_copies = []
    for c in sib_copies:
        c.wait()
    for r in range(2):
        both = hown[r] + sb[r].astype(F32)
        hown[r] = both
        hb[r] = both.astype(BF16)
    for d in others_z:
        to = lax.rem(z + d, 8)
        src = hb.at[lax.rem(to, 2), lax.div(to, 2)]
        z_copies.append(copy(src, rzs.at[d], w_s.at[1, d], w_r.at[1, d], at_z(d)))
    caption_part((3, 0))
    for c in back:
        c.wait()

    def ordered(v):
        tiles = [v[:, 128 * i:128 * i + 128] for i in range(4)]
        tails = [v[:, 512 + 64 * i:576 + 64 * i] for i in range(4)]
        return jnp.concatenate([t for pair in zip(tiles, tails) for t in pair], axis=1)

    acc = pc[x]
    for n in range(1, 16):
        acc = acc + got[n].astype(F32)
    held = hcap[...]
    clip_held = hclip[...]
    clip_unit = clip_held.astype(BF16).astype(F32)
    cap_unit = held.astype(BF16).astype(F32)
    pool_unit = pu[home, rows, :]
    grad = scale * acc - 0.5 * scale * clip_unit - 0.5 * scale * pool_unit
    dcap_ref[...] = ordered(
        (grad - held * jnp.sum(held * grad, axis=1, keepdims=True)) / hlen[1]
    )

    for c in z_copies:
        c.wait()
    acc = hown[zl, zh]
    for d in range(1, 8):
        acc = acc + rzs[d].astype(F32)
    grad = scale * acc - 0.5 * scale * cap_unit
    dclip_ref[...] = ordered(
        (grad - clip_held * jnp.sum(clip_held * grad, axis=1, keepdims=True)) / hlen[0]
    )


def body(clips, captions, video_id, logit_scale):
    vmem = pl.BlockSpec(memory_space=pltpu.VMEM)
    hbm = pl.BlockSpec(memory_space=pltpu.HBM)
    dma = lambda *shape: pltpu.SemaphoreType.DMA(shape)
    out = jax.ShapeDtypeStruct((32, 768), F32)
    V = pltpu.VMEM
    keep = lambda v: pltpu.with_memory_space_constraint(v, pltpu.HBM)
    return pl.pallas_call(
        kernel,
        out_shape=(out, out),
        in_specs=[pl.BlockSpec(memory_space=pltpu.SMEM), hbm, hbm, hbm],
        out_specs=(vmem, vmem),
        scratch_shapes=[
            V((2, 192, 128), BF16), V((64, 128), jnp.int32),
            V((4, 48, 128), BF16), V((4, 48, 128), BF16), V((16, 192, 128), BF16),
            V((32, 768), F32), V((32, 768), F32), V((2, 32, 1), F32),
            V((768, 512), BF16), V((16, 32, 768), BF16),
            V((4, 128, 1), F32), V((1, 512), F32), V((1, 512), F32), V((4, 128, 1), F32),
            V((4, 128, 768), F32), V((4, 128, 1), F32), V((4, 1, 768), F32), V((4, 1, 768), F32),
            V((4, 128, 512), F32), V((4, 128, 512), F32), V((512, 512), F32), V((512, 512), F32),
            V((4, 128, 768), F32),
            V((8, 128), F32), V((16, 8, 128), F32), V((8, 128), F32), V((16, 8, 128), F32),
            V((2, 4, 32, 768), BF16), V((2, 4, 32, 768), BF16), V((2, 4, 32, 768), BF16),
            V((2, 4, 32, 768), F32), V((8, 32, 768), BF16),
            V((4, 32, 768), F32), V((4, 4, 32, 768), BF16), V((16, 32, 768), BF16),
            dma(3), dma(4), dma(4), dma(8), dma(8), dma(8), dma(8), dma(4, 4), dma(4, 4),
            dma(4), dma(4), dma(2, 16), dma(2, 16), dma(2, 8), dma(2, 8), dma(4, 4), dma(4, 4),
        ],
        compiler_params=pltpu.CompilerParams(
            collective_id=0, has_side_effects=True, vmem_limit_bytes=48 * 1024 * 1024
        ),
        name="contrastive",
    )(logit_scale.reshape(1), keep(video_id.reshape(64, 128)), keep(clips.T), keep(captions.T))


def solution(mesh):
    in_specs = (P("dp", "mp"), P("dp", "mp"), P(), P())
    out_specs = (P(("dp", "mp"), None), P(("dp", "mp"), None))
    return jax.shard_map(body, mesh=mesh, in_specs=in_specs, out_specs=out_specs, check_vma=False)
```

```python
import jax
import jax.numpy as jnp
from jax import lax
from jax.experimental import pallas as pl
from jax.experimental.pallas import tpu as pltpu
from jax.sharding import PartitionSpec as P

EPSILON = 1e-06
NEGATIVE_FILL = -1e30
F32 = jnp.float32
BF16 = jnp.bfloat16
MESH = pl.DeviceIdType.MESH


def chip(x, y, z, core):
    return ((y * 2 + lax.rem(z, 2)) * 8 + x * 2 + core, lax.div(z, 2))


def kernel(
    scale_ref, vid_ref, clips_ref, caps_ref,
    dclip_ref, dcap_ref,
    raw, vid, pkt, ta, cr, hcap, hclip, hlen,
    clt, ct, vic, vjr, vir, vjc,
    pu, plen, eo, ei,
    ej, ek, ejt, ekt, pj, ctop,
    rst, rz, cst, cz,
    g, sb, hb, hown, s1, s1h, m1, m2, r1z, r2z,
    g2, pc, qy, qx, r0, r1, r0b, r1b, fx, fy,
    l_s, a2a_s, a2a_r, z_s, z_r, s_s, s_r, p_s, p_r, f_s, f_r, e_s, e_r,
    t_s, t_r, w_s, w_r, x_s, x_r, v_s, v_r,
):
    dp = lax.axis_index("dp")
    zh = lax.axis_index("mp")
    core = lax.rem(dp, 2)
    x = lax.rem(lax.div(dp, 2), 4)
    zl = lax.rem(lax.div(dp, 8), 2)
    y = lax.div(dp, 16)
    z = zh * 2 + zl
    home = zl * 2 + core
    sibling = chip(x, y, z, 1 - core)
    at_z = lambda d: chip(x, y, lax.rem(z + d, 8), core)
    at_x = lambda d: chip(lax.rem(x + d, 4), y, z, core)
    at_y = lambda d: chip(x, lax.rem(y + d, 4), z, core)

    others_z = (4, 3, 5, 2, 6, 1, 7)
    others_xy = sorted(
        [(i, j) for i in range(4) for j in range(4) if i or j],
        key=lambda t: -(min(t[0], 4 - t[0]) + min(t[1], 4 - t[1])),
    )
    at_xy = lambda i, j: chip(lax.rem(x + i, 4), lax.rem(y + j, 4), z, core)

    def copy(src, dst, send, recv, device):
        c = pltpu.make_async_remote_copy(
            src_ref=src, dst_ref=dst, send_sem=send, recv_sem=recv,
            device_id=device, device_id_type=MESH,
        )
        c.start()
        return c

    runs = [y * 8 + x, y * 8 + 4 + x]

    def owner(q):
        return chip(lax.rem(q, 4), lax.div(q, 8), z, core), lax.rem(lax.div(q, 4), 2)

    after = [owner(lax.rem(q + 1, 32)) for q in runs]
    before = [owner(lax.rem(q + 31, 32)) for q in runs]

    barrier = pltpu.get_barrier_semaphore()
    partners = [at_z(d) for d in others_z]
    partners += [chip(x, y, lax.rem(z + d, 8), 1 - core) for d in others_z]
    partners += [at_xy(i, j) for i, j in others_xy] + [sibling]
    for device in partners:
        pl.semaphore_signal(barrier, inc=1, device_id=device, device_id_type=MESH)
    loads = [
        pltpu.make_async_copy(src, dst, l_s.at[i])
        for i, (src, dst) in enumerate(((caps_ref, raw.at[1]), (clips_ref, raw.at[0]), (vid_ref, vid)))
    ]
    for c in loads:
        c.start()

    loads[0].wait()
    block = raw[1].astype(F32).T
    for k in range(4):
        pkt[k, 0:32] = block[32 * k:32 * k + 32, 0:128].astype(BF16)
        tail = block[32 * k:32 * k + 32, 128:192]
        pkt[k, 32:48] = jnp.concatenate([tail[0:16], tail[16:32]], axis=1).astype(BF16)
    ta[zh] = pkt[zh]
    loads[1].wait()
    slot = lambda at, c: lax.rem(at, 2) * 8 + c * 4 + lax.div(at, 2)
    mine = slot(z, core)
    cr[mine] = raw[0]

    loads[2].wait()
    sub = lax.broadcasted_iota(jnp.int32, (128, 128), 0)
    lane = lax.broadcasted_iota(jnp.int32, (128, 128), 1)
    eye = sub == lane

    def to_col(row):
        return jnp.sum(jnp.where(eye, row, 0.0), axis=1, keepdims=True)

    def to_row(col):
        return jnp.sum(jnp.where(eye, col, 0.0), axis=0, keepdims=True)

    def block_of(b):
        return (y * 2 + lax.div(b, 2)) * 8 + x * 2 + lax.rem(b, 2)

    def ids_of(row):
        return vid[pl.ds(row, 1), :].astype(F32)

    for b in range(4):
        ids = ids_of(block_of(b))
        vir[:, 128 * b:128 * b + 128] = ids
        vic[b] = to_col(ids)
    segment = lax.div(lax.broadcasted_iota(jnp.int32, (1, 128), 1), 16)
    for h in range(2):
        for grp in range(2):
            out = jnp.zeros((1, 128), F32)
            for s in range(8):
                a, b = grp * 2 + s // 4, s % 4
                ys, xs = (a, b) if h == 0 else (b, a)
                v = ids_of((ys * 2 + zl) * 8 + xs * 2 + core)
                shift = lax.rem(s * 16 + 256 - zh * 32 - h * 16, 128)
                out = jnp.where(segment == s, pltpu.roll(v, shift, 1), out)
            vjr[:, (h * 2 + grp) * 128:(h * 2 + grp + 1) * 128] = out
            vjc[h * 2 + grp] = to_col(out)

    pl.semaphore_wait(barrier, len(partners))

    pending = []
    for d in (2, 1, 3):
        to = lax.rem(zh + d, 4)
        pending.append(copy(pkt.at[to], ta.at[zh], a2a_s.at[d], a2a_r.at[d], (dp, to)))
    own = raw.at[0]
    sib_copies = [copy(own, cr.at[mine], s_s.at[0], s_r.at[0], sibling)]
    near = {d: copy(own, cr.at[mine], z_s.at[d], z_r.at[d], at_z(d)) for d in (1, 7, 2, 6)}

    def to_sibling(d):
        ref = cr.at[slot(lax.rem(z + 8 - d, 8), core)]
        sib_copies.append(copy(ref, ref, s_s.at[d], s_r.at[d], sibling))

    far = {}

    def relay(d, to, sem, rows):
        near[d].wait()
        at = slot(lax.rem(z + 8 - d, 8), core)
        ref = cr.at[at] if rows is None else cr.at[at, pl.ds(rows, 96)]
        far[sem] = copy(ref, ref, z_s.at[sem], z_r.at[sem], at_z(to))
        to_sibling(d)

    relay(1, 2, 3, None)
    relay(7, 6, 5, None)

    def unpacked(parts):
        low = lax.broadcasted_iota(jnp.int32, (16, 128), 1) < 64
        tiles = [p[0:32].astype(F32) for p in parts]
        tails = [p[32:48].astype(F32) for p in parts]
        for i in (0, 2):
            left, right = tails[i], tails[i + 1]
            upper = jnp.where(low, left, pltpu.roll(right, 64, 1))
            lower = jnp.where(low, pltpu.roll(left, 64, 1), right)
            tiles.append(jnp.concatenate([upper, lower], axis=0))
        return jnp.concatenate(tiles, axis=1)

    def lengths(full):
        return jnp.sqrt(jnp.sum(full * full, axis=1, keepdims=True) + EPSILON)

    for c in pending:
        c.wait()
    full = unpacked([ta[k] for k in range(4)])
    length = lengths(full)
    full = full / length
    hcap[...] = full
    hlen[1] = length
    u = full.astype(BF16)
    ct[0, y, x] = u[0:16]
    ct[1, x, y] = u[16:32]
    axes = ((at_x, at_y, y, x), (at_y, at_x, x, y))
    stage_a = [[], []]
    for d in (2, 1, 3):
        for h, (along, _, i, j) in enumerate(axes):
            ref = ct.at[h, i, j]
            stage_a[h].append((d, copy(ref, ref, p_s.at[h, d], p_r.at[h, d], along(d))))
    stage_b = []

    def forward(h, e):
        _, across, i, j = axes[h]
        ref = ct.at[h, i, lax.rem(j + 4 - e, 4)]
        for d in (2, 1, 3):
            stage_b.append(copy(ref, ref, f_s.at[h, e, d], f_r.at[h, e, d], across(d)))

    forward(0, 0)
    forward(1, 0)
    relay(2, 2, 4, 0)
    relay(6, 6, 0, 96)
    for n in (1, 2, 0):
        for h in range(2):
            d, c = stage_a[h][n]
            c.wait()
            forward(h, d)
    for d in (3, 5):
        far[d].wait()
        to_sibling(d)
    far[4].wait()
    far[0].wait()
    to_sibling(4)
    for c in sib_copies:
        c.wait()

    def normalise(b, carry):
        parts = [cr[4 * b + k].astype(F32) for k in range(4)]
        total = sum(jnp.sum(p * p, axis=0, keepdims=True) for p in parts)
        inverse = 1.0 / jnp.sqrt(total + EPSILON)
        columns = pl.ds(pl.multiple_of(128 * b, 128), 128)
        for k, p in enumerate(parts):
            p = (p * inverse).astype(BF16)
            clt[128 * k:128 * k + 128, columns] = p[0:128]
            clt[512 + 64 * k:576 + 64 * k, columns] = p[128:192]
        return carry

    lax.fori_loop(0, 4, normalise, 0)

    edge_copies = []
    for r in range(2):
        ids = vir[:, 256 * r:256 * r + 256]
        col = jnp.concatenate([vic[2 * r], vic[2 * r + 1]], axis=0)
        alike = jnp.where(col == ids, 1.0, 0.0).astype(BF16)
        local = lax.dot_general(
            alike, clt[:, 256 * r:256 * r + 256], (((1,), (1,)), ((), ())),
            preferred_element_type=F32,
        )
        pu[2 * r] = local[0:128]
        pu[2 * r + 1] = local[128:256]
        eo[2 * r] = local[0:1]
        eo[2 * r + 1] = local[255:256]
        device, side = before[r]
        edge_copies.append(
            copy(eo.at[2 * r], ei.at[side * 2 + 1], e_s.at[2 * r], e_r.at[side * 2 + 1], device)
        )
        device, side = after[r]
        edge_copies.append(
            copy(eo.at[2 * r + 1], ei.at[side * 2], e_s.at[2 * r + 1], e_r.at[side * 2], device)
        )
    for c in stage_b:
        c.wait()

    scale = scale_ref[0]
    ej[...] = jnp.dot(
        ct[...].reshape(512, 768), clt[...], preferred_element_type=F32
    ).reshape(4, 128, 512)
    column = lax.broadcasted_iota(jnp.int32, (1, 512), 1)
    clip_pos = (y * 2 + lax.div(column, 256)) * 1024 + x * 256 + lax.rem(column, 256)

    def pass_one(b, top):
        j = b * 128 + lax.broadcasted_iota(jnp.int32, (128, 1), 0)
        half = lax.div(j, 256)
        first = lax.rem(lax.div(j, 64), 4)
        second = lax.rem(lax.div(j, 16), 4)
        ypos = jnp.where(half == 0, first, second)
        xpos = jnp.where(half == 0, second, first)
        cap_pos = ((ypos * 2 + zl) * 8 + xpos * 2 + core) * 128 + zh * 32 + half * 16 + lax.rem(j, 16)
        alike = vjc[b] == vir[...]
        allowed = jnp.logical_not(alike) | (cap_pos == clip_pos)
        s = jnp.where(allowed, scale * ej[b], NEGATIVE_FILL)
        ek[b] = s
        high = jnp.max(s, axis=1, keepdims=True)
        e = jnp.exp(s - high)
        ej[b] = e
        high = to_row(high)
        ctop[pl.ds(b, 1), :] = high
        cst[pl.ds(b, 1), :] = high + jnp.log(to_row(jnp.sum(e, axis=1, keepdims=True)))
        return jnp.maximum(top, jnp.max(s, axis=0, keepdims=True))

    clip_top = lax.fori_loop(0, 4, pass_one, jnp.full((1, 512), NEGATIVE_FILL, F32))
    stats = []
    for i, j in others_xy:
        n = i * 4 + j
        stats.append(copy(cst, cz.at[n], t_s.at[1, n], t_r.at[1, n], at_xy(i, j)))

    def pass_two(b, total):
        e = jnp.exp(ek[b] - clip_top)
        ek[b] = e
        return total + jnp.sum(e, axis=0, keepdims=True)

    clip_lse = clip_top + jnp.log(lax.fori_loop(0, 4, pass_two, jnp.zeros((1, 512), F32)))
    for b in range(4):
        rst[b:b + 1, :] = clip_lse[:, b * 128:(b + 1) * 128]
    for d in others_z + (0,):
        for i in range(2):
            if d or i:
                n = i * 8 + d
                device = chip(x, y, lax.rem(z + d, 8), core if i == 0 else 1 - core)
                stats.append(copy(rst, rz.at[n], t_s.at[0, n], t_r.at[0, n], device))
    rz[0] = rst[...]
    cz[0] = cst[...]

    def joined(ref):
        values = ref[...]
        top = jnp.max(values, axis=0)
        return top + jnp.log(jnp.sum(jnp.exp(values - top), axis=0))

    for b in range(4):
        ejt[:, b * 128:(b + 1) * 128] = ej[b].T
        ekt[:, b * 128:(b + 1) * 128] = ek[b].T
    parts = [cr[4 * home + k].astype(F32) for k in range(4)]
    full = jnp.concatenate([p[0:128] for p in parts] + [p[128:192] for p in parts], axis=0)
    pj[0] = full.T
    rows = pl.ds(pl.multiple_of(zh * 32, 32), 32)
    full = pj[0, rows, :]
    length = lengths(full)
    hclip[...] = full / length
    hlen[0] = length
    for c in edge_copies:
        c.wait()
    for b in range(4):
        r = b // 2
        q = runs[r]
        left = ids_of(jnp.maximum(2 * q - 1, 0))[:, 127:128]
        right = ids_of(jnp.minimum(2 * q + 2, 63))[:, 0:1]
        from_left = jnp.where(vic[b] == left, jnp.where(q > 0, 1.0, 0.0), 0.0)
        from_right = jnp.where(vic[b] == right, jnp.where(q < 31, 1.0, 0.0), 0.0)
        pooled = pu[b] + from_left * ei[2 * r] + from_right * ei[2 * r + 1]
        length = lengths(pooled)
        plen[b] = length
        pu[b] = pooled * (1.0 / length)

    def projected(b, carry):
        alike = jnp.where(vic[b] == vjr[...], 1.0, 0.0).astype(BF16)
        acc = jnp.dot(alike, ct[...].reshape(512, 768), preferred_element_type=F32)
        pool = pu[b]
        acc = acc - pool * jnp.sum(pool * acc, axis=1, keepdims=True)
        pj[b] = acc * (0.5 / plen[b])
        return carry

    lax.fori_loop(0, 4, projected, 0)

    for c in stats:
        c.wait()
    whole = joined(rz)
    whole = jnp.concatenate([whole[b:b + 1] for b in range(4)], axis=1)
    clip_line = 0.5 * jnp.exp(clip_top - whole)
    for b in range(4):
        rst[b:b + 1, :] = clip_line[:, b * 128:(b + 1) * 128]
    cap_fac = 0.5 * jnp.exp(ctop[...] - joined(cz))
    cap_line = jnp.concatenate([cap_fac[b:b + 1] for b in range(4)], axis=1)

    def weigh(c):
        blocks = [c, 2 + c]
        w = []
        for b in blocks:
            rows = pl.ds(pl.multiple_of(128 * b, 128), 128)
            w.append(
                (ekt[rows, :] * to_col(rst[pl.ds(b, 1), :]) + ejt[rows, :] * cap_line).astype(BF16)
            )
        part = jnp.dot(
            jnp.concatenate(w, axis=0), ct[...].reshape(512, 768), preferred_element_type=F32
        )
        return [part[128 * i:128 * i + 128] - pj[b] for i, b in enumerate(blocks)]

    sib_copies = []
    for r, part in enumerate(weigh(1 - core)):
        g[r] = part.astype(BF16).reshape(4, 32, 768)
        sib_copies.append(copy(g.at[r], sb.at[r], w_s.at[0, r], w_r.at[0, r], sibling))

    stage_a = []

    def caption_part(h):
        w = [
            (ek[b] * clip_line + ej[b] * to_col(cap_fac[b:b + 1])).astype(BF16)
            for b in (2 * h, 2 * h + 1)
        ]
        part = lax.dot_general(
            jnp.concatenate(w, axis=0), clt[...], (((1,), (1,)), ((), ())),
            preferred_element_type=F32,
        ).reshape(4, 4, 16, 768)
        pc[h] = part
        g2[h] = part.astype(BF16)
        at, to, first = ((at_y, qy, y), (at_x, qx, x))[h]
        for d in (2, 1, 3):
            src = g2.at[h, lax.rem(first + d, 4)]
            stage_a.append(copy(src, to.at[d], v_s.at[h, d], v_r.at[h, d], at(d)))

    caption_part(0)
    caption_part(1)
    for r, part in enumerate(weigh(core)):
        hown[r] = part.reshape(4, 32, 768)

    for c in sib_copies:
        c.wait()
    for r in range(2):
        both = hown[r] + sb[r].astype(F32)
        hown[r] = both
        hb[r] = both.astype(BF16)

    def piece(d):
        to = lax.rem(z + d, 8)
        return lax.rem(to, 2), lax.div(to, 2)

    upper, lower = pl.ds(0, 16), pl.ds(16, 16)
    first = []
    z_copies = []
    for n, (to, d) in enumerate(((2, 3), (6, 5))):
        first.append(
            copy(hb.at[piece(d)], s1.at[n], x_s.at[0, n], x_r.at[0, n], at_z(to))
        )
    for n, (to, rows16) in enumerate(((2, upper), (6, lower))):
        first.append(
            copy(hb.at[(*piece(4), rows16)], s1h.at[n], x_s.at[1, n], x_r.at[1, n], at_z(to))
        )
    for n, (to, rows16) in enumerate(((2, lower), (6, upper))):
        z_copies.append(
            copy(hb.at[(*piece(to), rows16)], r2z.at[n, rows16], x_s.at[2, n], x_r.at[2, n], at_z(to))
        )
    for n, d in enumerate((1, 7)):
        first[n].wait()
        a, b = piece(d)
        m1[n] = (hown[a, b] + s1[n].astype(F32)).astype(BF16)
        z_copies.append(copy(m1.at[n], r1z.at[n], x_s.at[3, n], x_r.at[3, n], at_z(d)))
    for n, (d, rows16) in enumerate(((2, upper), (6, lower))):
        first[2 + n].wait()
        a, b = piece(d)
        m2[n] = (hown[a, b, rows16] + s1h[n].astype(F32)).astype(BF16)
        z_copies.append(
            copy(m2.at[n], r2z.at[n, rows16], x_s.at[4, n], x_r.at[4, n], at_z(d))
        )

    stage_b = []
    for c in stage_a[:3]:
        c.wait()
    total = pc[0, y] + qy[1].astype(F32) + qy[2].astype(F32) + qy[3].astype(F32)
    r0[...] = total
    r0b[...] = total.astype(BF16)
    for d in (2, 1, 3):
        src = r0b.at[lax.rem(x + d, 4)]
        stage_b.append(copy(src, fx.at[d], v_s.at[2, d], v_r.at[2, d], at_x(d)))
    for c in stage_a[3:]:
        c.wait()
    total = pc[1, x] + qx[1].astype(F32) + qx[2].astype(F32) + qx[3].astype(F32)
    r1[...] = total
    r1b[...] = total.astype(BF16)
    for d in (2, 1, 3):
        src = r1b.at[lax.rem(y + d, 4)]
        stage_b.append(copy(src, fy.at[d], v_s.at[3, d], v_r.at[3, d], at_y(d)))
    for c in stage_b:
        c.wait()

    def ordered(v):
        tiles = [v[:, 128 * i:128 * i + 128] for i in range(4)]
        tails = [v[:, 512 + 64 * i:576 + 64 * i] for i in range(4)]
        return jnp.concatenate([t for pair in zip(tiles, tails) for t in pair], axis=1)

    low = r0[x] + fx[1].astype(F32) + fx[2].astype(F32) + fx[3].astype(F32)
    high = r1[y] + fy[1].astype(F32) + fy[2].astype(F32) + fy[3].astype(F32)
    acc = jnp.concatenate([low, high], axis=0)
    held = hcap[...]
    clip_held = hclip[...]
    clip_unit = clip_held.astype(BF16).astype(F32)
    cap_unit = held.astype(BF16).astype(F32)
    pool_unit = pu[home, rows, :]
    grad = scale * acc - 0.5 * scale * clip_unit - 0.5 * scale * pool_unit
    dcap_ref[...] = ordered(
        (grad - held * jnp.sum(held * grad, axis=1, keepdims=True)) / hlen[1]
    )

    for c in z_copies:
        c.wait()
    acc = hown[zl, zh] + r1z[0].astype(F32) + r1z[1].astype(F32)
    acc = acc + r2z[0].astype(F32) + r2z[1].astype(F32)
    grad = scale * acc - 0.5 * scale * cap_unit
    dclip_ref[...] = ordered(
        (grad - clip_held * jnp.sum(clip_held * grad, axis=1, keepdims=True)) / hlen[0]
    )


def body(clips, captions, video_id, logit_scale):
    vmem = pl.BlockSpec(memory_space=pltpu.VMEM)
    hbm = pl.BlockSpec(memory_space=pltpu.HBM)
    dma = lambda *shape: pltpu.SemaphoreType.DMA(shape)
    out = jax.ShapeDtypeStruct((32, 768), F32)
    V = pltpu.VMEM
    keep = lambda v: pltpu.with_memory_space_constraint(v, pltpu.HBM)
    return pl.pallas_call(
        kernel,
        out_shape=(out, out),
        in_specs=[pl.BlockSpec(memory_space=pltpu.SMEM), hbm, hbm, hbm],
        out_specs=(vmem, vmem),
        scratch_shapes=[
            V((2, 192, 128), BF16), V((64, 128), jnp.int32),
            V((4, 48, 128), BF16), V((4, 48, 128), BF16), V((16, 192, 128), BF16),
            V((32, 768), F32), V((32, 768), F32), V((2, 32, 1), F32),
            V((768, 512), BF16), V((2, 4, 4, 16, 768), BF16),
            V((4, 128, 1), F32), V((1, 512), F32), V((1, 512), F32), V((4, 128, 1), F32),
            V((4, 128, 768), F32), V((4, 128, 1), F32), V((4, 1, 768), F32), V((4, 1, 768), F32),
            V((4, 128, 512), F32), V((4, 128, 512), F32), V((512, 512), F32), V((512, 512), F32),
            V((4, 128, 768), F32), V((4, 128), F32),
            V((4, 128), F32), V((16, 4, 128), F32), V((4, 128), F32), V((16, 4, 128), F32),
            V((2, 4, 32, 768), BF16), V((2, 4, 32, 768), BF16), V((2, 4, 32, 768), BF16),
            V((2, 4, 32, 768), F32), V((2, 32, 768), BF16), V((2, 16, 768), BF16),
            V((2, 32, 768), BF16), V((2, 16, 768), BF16), V((2, 32, 768), BF16),
            V((2, 32, 768), BF16),
            V((2, 4, 4, 16, 768), BF16), V((2, 4, 4, 16, 768), F32),
            V((4, 4, 16, 768), BF16), V((4, 4, 16, 768), BF16),
            V((4, 16, 768), F32), V((4, 16, 768), F32),
            V((4, 16, 768), BF16), V((4, 16, 768), BF16),
            V((4, 16, 768), BF16), V((4, 16, 768), BF16),
            dma(3), dma(4), dma(4), dma(8), dma(8), dma(8), dma(8), dma(2, 4), dma(2, 4),
            dma(2, 4, 4), dma(2, 4, 4),
            dma(4), dma(4), dma(2, 16), dma(2, 16), dma(1, 2), dma(1, 2), dma(5, 2), dma(5, 2),
            dma(4, 4), dma(4, 4),
        ],
        compiler_params=pltpu.CompilerParams(
            collective_id=0, has_side_effects=True, vmem_limit_bytes=48 * 1024 * 1024
        ),
        name="contrastive",
    )(logit_scale.reshape(1), keep(video_id.reshape(64, 128)), keep(clips.T), keep(captions.T))


def solution(mesh):
    in_specs = (P("dp", "mp"), P("dp", "mp"), P(), P())
    out_specs = (P(("dp", "mp"), None), P(("dp", "mp"), None))
    return jax.shard_map(body, mesh=mesh, in_specs=in_specs, out_specs=out_specs, check_vma=False)
```

```python
import jax
import jax.numpy as jnp
from jax import lax
from jax.experimental import pallas as pl
from jax.experimental.pallas import tpu as pltpu
from jax.sharding import PartitionSpec as P

EPSILON = 1e-06
NEGATIVE_FILL = -1e30
F32 = jnp.float32
BF16 = jnp.bfloat16
MESH = pl.DeviceIdType.MESH


def chip(x, y, z, core):
    return ((y * 2 + lax.rem(z, 2)) * 8 + x * 2 + core, lax.div(z, 2))


def kernel(
    scale_ref, vid_ref, clips_ref, caps_ref,
    dclip_ref, dcap_ref,
    raw, vid, pkt, ta, cr, hcap, hclip, hlen,
    clt, ct, vic, vjr, vir, vjc,
    pu, plen, eo, ei,
    ej, ek, ejt, ekt, pj, ctop,
    rst, rz, cst, cz,
    g, sb, hb, hown, s1, s1h, m1, m2, r1z, r2z,
    g2, pc, qy, qx, r0, r1, r0b, r1b, fx, fy,
    l_s, a2a_s, a2a_r, z_s, z_r, s_s, s_r, p_s, p_r, f_s, f_r, e_s, e_r,
    t_s, t_r, w_s, w_r, x_s, x_r, v_s, v_r,
):
    dp = lax.axis_index("dp")
    zh = lax.axis_index("mp")
    core = lax.rem(dp, 2)
    x = lax.rem(lax.div(dp, 2), 4)
    zl = lax.rem(lax.div(dp, 8), 2)
    y = lax.div(dp, 16)
    z = zh * 2 + zl
    home = zl * 2 + core
    sibling = chip(x, y, z, 1 - core)
    at_z = lambda d: chip(x, y, lax.rem(z + d, 8), core)
    at_x = lambda d: chip(lax.rem(x + d, 4), y, z, core)
    at_y = lambda d: chip(x, lax.rem(y + d, 4), z, core)

    others_z = (4, 3, 5, 2, 6, 1, 7)
    others_xy = sorted(
        [(i, j) for i in range(4) for j in range(4) if i or j],
        key=lambda t: -(min(t[0], 4 - t[0]) + min(t[1], 4 - t[1])),
    )
    at_xy = lambda i, j: chip(lax.rem(x + i, 4), lax.rem(y + j, 4), z, core)

    def copy(src, dst, send, recv, device):
        c = pltpu.make_async_remote_copy(
            src_ref=src, dst_ref=dst, send_sem=send, recv_sem=recv,
            device_id=device, device_id_type=MESH,
        )
        c.start()
        return c

    runs = [y * 8 + x, y * 8 + 4 + x]

    def owner(q):
        return chip(lax.rem(q, 4), lax.div(q, 8), z, core), lax.rem(lax.div(q, 4), 2)

    after = [owner(lax.rem(q + 1, 32)) for q in runs]
    before = [owner(lax.rem(q + 31, 32)) for q in runs]

    barrier = pltpu.get_barrier_semaphore()
    partners = [at_z(d) for d in others_z]
    partners += [chip(x, y, lax.rem(z + d, 8), 1 - core) for d in others_z]
    partners += [at_xy(i, j) for i, j in others_xy] + [sibling]
    for device in partners:
        pl.semaphore_signal(barrier, inc=1, device_id=device, device_id_type=MESH)
    loads = [
        pltpu.make_async_copy(src, dst, l_s.at[i])
        for i, (src, dst) in enumerate(((caps_ref, raw.at[1]), (clips_ref, raw.at[0]), (vid_ref, vid)))
    ]
    for c in loads:
        c.start()

    loads[0].wait()
    block = raw[1].astype(F32).T
    for k in range(4):
        pkt[k, 0:32] = block[32 * k:32 * k + 32, 0:128].astype(BF16)
        tail = block[32 * k:32 * k + 32, 128:192]
        pkt[k, 32:48] = jnp.concatenate([tail[0:16], tail[16:32]], axis=1).astype(BF16)
    ta[zh] = pkt[zh]
    loads[1].wait()
    slot = lambda at, c: lax.rem(at, 2) * 8 + c * 4 + lax.div(at, 2)
    mine = slot(z, core)
    cr[mine] = raw[0]

    loads[2].wait()
    sub = lax.broadcasted_iota(jnp.int32, (128, 128), 0)
    lane = lax.broadcasted_iota(jnp.int32, (128, 128), 1)
    eye = sub == lane

    def to_col(row):
        return jnp.sum(jnp.where(eye, row, 0.0), axis=1, keepdims=True)

    def to_row(col):
        return jnp.sum(jnp.where(eye, col, 0.0), axis=0, keepdims=True)

    def block_of(b):
        return (y * 2 + lax.div(b, 2)) * 8 + x * 2 + lax.rem(b, 2)

    def ids_of(row):
        return vid[pl.ds(row, 1), :].astype(F32)

    for b in range(4):
        ids = ids_of(block_of(b))
        vir[:, 128 * b:128 * b + 128] = ids
        vic[b] = to_col(ids)
    segment = lax.div(lax.broadcasted_iota(jnp.int32, (1, 128), 1), 16)
    for h in range(2):
        for grp in range(2):
            out = jnp.zeros((1, 128), F32)
            for s in range(8):
                a, b = grp * 2 + s // 4, s % 4
                ys, xs = (a, b) if h == 0 else (b, a)
                v = ids_of((ys * 2 + zl) * 8 + xs * 2 + core)
                shift = lax.rem(s * 16 + 256 - zh * 32 - h * 16, 128)
                out = jnp.where(segment == s, pltpu.roll(v, shift, 1), out)
            vjr[:, (h * 2 + grp) * 128:(h * 2 + grp + 1) * 128] = out
            vjc[h * 2 + grp] = to_col(out)

    pl.semaphore_wait(barrier, len(partners))

    pending = []
    for d in (2, 1, 3):
        to = lax.rem(zh + d, 4)
        pending.append(copy(pkt.at[to], ta.at[zh], a2a_s.at[d], a2a_r.at[d], (dp, to)))
    own = raw.at[0]
    sib_copies = [copy(own, cr.at[mine], s_s.at[0], s_r.at[0], sibling)]
    near = {d: copy(own, cr.at[mine], z_s.at[d], z_r.at[d], at_z(d)) for d in (1, 7, 2, 6)}

    def to_sibling(d):
        ref = cr.at[slot(lax.rem(z + 8 - d, 8), core)]
        sib_copies.append(copy(ref, ref, s_s.at[d], s_r.at[d], sibling))

    far = {}

    def relay(d, to, sem, rows):
        near[d].wait()
        at = slot(lax.rem(z + 8 - d, 8), core)
        ref = cr.at[at] if rows is None else cr.at[at, pl.ds(rows, 96)]
        far[sem] = copy(ref, ref, z_s.at[sem], z_r.at[sem], at_z(to))
        to_sibling(d)


    def unpacked(parts):
        low = lax.broadcasted_iota(jnp.int32, (16, 128), 1) < 64
        tiles = [p[0:32].astype(F32) for p in parts]
        tails = [p[32:48].astype(F32) for p in parts]
        for i in (0, 2):
            left, right = tails[i], tails[i + 1]
            upper = jnp.where(low, left, pltpu.roll(right, 64, 1))
            lower = jnp.where(low, pltpu.roll(left, 64, 1), right)
            tiles.append(jnp.concatenate([upper, lower], axis=0))
        return jnp.concatenate(tiles, axis=1)

    def lengths(full):
        return jnp.sqrt(jnp.sum(full * full, axis=1, keepdims=True) + EPSILON)

    for c in pending:
        c.wait()
    full = unpacked([ta[k] for k in range(4)])
    length = lengths(full)
    full = full / length
    hcap[...] = full
    hlen[1] = length
    u = full.astype(BF16)
    ct[0, y, x] = u[0:16]
    ct[1, x, y] = u[16:32]
    axes = ((at_x, at_y, y, x), (at_y, at_x, x, y))
    stage_a = [[], []]
    for d in (2, 1, 3):
        for h, (along, _, i, j) in enumerate(axes):
            ref = ct.at[h, i, j]
            stage_a[h].append((d, copy(ref, ref, p_s.at[h, d], p_r.at[h, d], along(d))))
    stage_b = []

    def forward(h, e):
        _, across, i, j = axes[h]
        ref = ct.at[h, i, lax.rem(j + 4 - e, 4)]
        for d in (2, 1, 3):
            stage_b.append(copy(ref, ref, f_s.at[h, e, d], f_r.at[h, e, d], across(d)))

    relay(1, 2, 3, None)
    relay(7, 6, 5, None)
    relay(2, 2, 4, 0)
    relay(6, 6, 0, 96)
    forward(0, 0)
    forward(1, 0)
    for n in (1, 2, 0):
        for h in range(2):
            d, c = stage_a[h][n]
            c.wait()
            forward(h, d)
    for d in (3, 5):
        far[d].wait()
        to_sibling(d)
    far[4].wait()
    far[0].wait()
    to_sibling(4)
    for c in sib_copies:
        c.wait()

    def normalise(b, carry):
        parts = [cr[4 * b + k].astype(F32) for k in range(4)]
        total = sum(jnp.sum(p * p, axis=0, keepdims=True) for p in parts)
        inverse = 1.0 / jnp.sqrt(total + EPSILON)
        columns = pl.ds(pl.multiple_of(128 * b, 128), 128)
        for k, p in enumerate(parts):
            p = (p * inverse).astype(BF16)
            clt[128 * k:128 * k + 128, columns] = p[0:128]
            clt[512 + 64 * k:576 + 64 * k, columns] = p[128:192]
        return carry

    lax.fori_loop(0, 4, normalise, 0)

    edge_copies = []
    for r in range(2):
        ids = vir[:, 256 * r:256 * r + 256]
        col = jnp.concatenate([vic[2 * r], vic[2 * r + 1]], axis=0)
        alike = jnp.where(col == ids, 1.0, 0.0).astype(BF16)
        local = lax.dot_general(
            alike, clt[:, 256 * r:256 * r + 256], (((1,), (1,)), ((), ())),
            preferred_element_type=F32,
        )
        pu[2 * r] = local[0:128]
        pu[2 * r + 1] = local[128:256]
        eo[2 * r] = local[0:1]
        eo[2 * r + 1] = local[255:256]
        device, side = before[r]
        edge_copies.append(
            copy(eo.at[2 * r], ei.at[side * 2 + 1], e_s.at[2 * r], e_r.at[side * 2 + 1], device)
        )
        device, side = after[r]
        edge_copies.append(
            copy(eo.at[2 * r + 1], ei.at[side * 2], e_s.at[2 * r + 1], e_r.at[side * 2], device)
        )
    for c in stage_b:
        c.wait()

    scale = scale_ref[0]
    ej[...] = jnp.dot(
        ct[...].reshape(512, 768), clt[...], preferred_element_type=F32
    ).reshape(4, 128, 512)
    column = lax.broadcasted_iota(jnp.int32, (1, 512), 1)
    clip_pos = (y * 2 + lax.div(column, 256)) * 1024 + x * 256 + lax.rem(column, 256)

    def pass_one(b, top):
        j = b * 128 + lax.broadcasted_iota(jnp.int32, (128, 1), 0)
        half = lax.div(j, 256)
        first = lax.rem(lax.div(j, 64), 4)
        second = lax.rem(lax.div(j, 16), 4)
        ypos = jnp.where(half == 0, first, second)
        xpos = jnp.where(half == 0, second, first)
        cap_pos = ((ypos * 2 + zl) * 8 + xpos * 2 + core) * 128 + zh * 32 + half * 16 + lax.rem(j, 16)
        alike = vjc[b] == vir[...]
        allowed = jnp.logical_not(alike) | (cap_pos == clip_pos)
        s = jnp.where(allowed, scale * ej[b], NEGATIVE_FILL)
        ek[b] = s
        high = jnp.max(s, axis=1, keepdims=True)
        e = jnp.exp(s - high)
        ej[b] = e
        high = to_row(high)
        ctop[pl.ds(b, 1), :] = high
        cst[pl.ds(b, 1), :] = high + jnp.log(to_row(jnp.sum(e, axis=1, keepdims=True)))
        return jnp.maximum(top, jnp.max(s, axis=0, keepdims=True))

    clip_top = lax.fori_loop(0, 4, pass_one, jnp.full((1, 512), NEGATIVE_FILL, F32))
    stats = []
    for i, j in others_xy:
        n = i * 4 + j
        stats.append(copy(cst, cz.at[n], t_s.at[1, n], t_r.at[1, n], at_xy(i, j)))

    def pass_two(b, total):
        e = jnp.exp(ek[b] - clip_top)
        ek[b] = e
        return total + jnp.sum(e, axis=0, keepdims=True)

    clip_lse = clip_top + jnp.log(lax.fori_loop(0, 4, pass_two, jnp.zeros((1, 512), F32)))
    for b in range(4):
        rst[b:b + 1, :] = clip_lse[:, b * 128:(b + 1) * 128]
    for d in others_z + (0,):
        for i in range(2):
            if d or i:
                n = i * 8 + d
                device = chip(x, y, lax.rem(z + d, 8), core if i == 0 else 1 - core)
                stats.append(copy(rst, rz.at[n], t_s.at[0, n], t_r.at[0, n], device))
    rz[0] = rst[...]
    cz[0] = cst[...]

    def joined(ref):
        values = ref[...]
        top = jnp.max(values, axis=0)
        return top + jnp.log(jnp.sum(jnp.exp(values - top), axis=0))

    for b in range(4):
        ejt[:, b * 128:(b + 1) * 128] = ej[b].T
        ekt[:, b * 128:(b + 1) * 128] = ek[b].T
    parts = [cr[4 * home + k].astype(F32) for k in range(4)]
    full = jnp.concatenate([p[0:128] for p in parts] + [p[128:192] for p in parts], axis=0)
    pj[0] = full.T
    rows = pl.ds(pl.multiple_of(zh * 32, 32), 32)
    full = pj[0, rows, :]
    length = lengths(full)
    hclip[...] = full / length
    hlen[0] = length
    for c in edge_copies:
        c.wait()
    for b in range(4):
        r = b // 2
        q = runs[r]
        left = ids_of(jnp.maximum(2 * q - 1, 0))[:, 127:128]
        right = ids_of(jnp.minimum(2 * q + 2, 63))[:, 0:1]
        from_left = jnp.where(vic[b] == left, jnp.where(q > 0, 1.0, 0.0), 0.0)
        from_right = jnp.where(vic[b] == right, jnp.where(q < 31, 1.0, 0.0), 0.0)
        pooled = pu[b] + from_left * ei[2 * r] + from_right * ei[2 * r + 1]
        length = lengths(pooled)
        plen[b] = length
        pu[b] = pooled * (1.0 / length)

    def projected(b, carry):
        alike = jnp.where(vic[b] == vjr[...], 1.0, 0.0).astype(BF16)
        acc = jnp.dot(alike, ct[...].reshape(512, 768), preferred_element_type=F32)
        pool = pu[b]
        acc = acc - pool * jnp.sum(pool * acc, axis=1, keepdims=True)
        pj[b] = acc * (0.5 / plen[b])
        return carry

    lax.fori_loop(0, 4, projected, 0)

    for c in stats:
        c.wait()
    whole = joined(rz)
    whole = jnp.concatenate([whole[b:b + 1] for b in range(4)], axis=1)
    clip_line = 0.5 * jnp.exp(clip_top - whole)
    for b in range(4):
        rst[b:b + 1, :] = clip_line[:, b * 128:(b + 1) * 128]
    cap_fac = 0.5 * jnp.exp(ctop[...] - joined(cz))
    cap_line = jnp.concatenate([cap_fac[b:b + 1] for b in range(4)], axis=1)

    def weigh(c):
        blocks = [c, 2 + c]
        w = []
        for b in blocks:
            rows = pl.ds(pl.multiple_of(128 * b, 128), 128)
            w.append(
                (ekt[rows, :] * to_col(rst[pl.ds(b, 1), :]) + ejt[rows, :] * cap_line).astype(BF16)
            )
        part = jnp.dot(
            jnp.concatenate(w, axis=0), ct[...].reshape(512, 768), preferred_element_type=F32
        )
        return [part[128 * i:128 * i + 128] - pj[b] for i, b in enumerate(blocks)]

    sib_copies = []
    for r, part in enumerate(weigh(1 - core)):
        g[r] = part.astype(BF16).reshape(4, 32, 768)
        sib_copies.append(copy(g.at[r], sb.at[r], w_s.at[0, r], w_r.at[0, r], sibling))

    stage_a = []

    def caption_part(h):
        w = [
            (ek[b] * clip_line + ej[b] * to_col(cap_fac[b:b + 1])).astype(BF16)
            for b in (2 * h, 2 * h + 1)
        ]
        part = lax.dot_general(
            jnp.concatenate(w, axis=0), clt[...], (((1,), (1,)), ((), ())),
            preferred_element_type=F32,
        ).reshape(4, 4, 16, 768)
        pc[h] = part
        g2[h] = part.astype(BF16)
        at, to, first = ((at_y, qy, y), (at_x, qx, x))[h]
        for d in (2, 1, 3):
            src = g2.at[h, lax.rem(first + d, 4)]
            stage_a.append(copy(src, to.at[d], v_s.at[h, d], v_r.at[h, d], at(d)))

    caption_part(0)
    caption_part(1)
    for r, part in enumerate(weigh(core)):
        hown[r] = part.reshape(4, 32, 768)

    for c in sib_copies:
        c.wait()
    for r in range(2):
        both = hown[r] + sb[r].astype(F32)
        hown[r] = both
        hb[r] = both.astype(BF16)

    def piece(d):
        to = lax.rem(z + d, 8)
        return lax.rem(to, 2), lax.div(to, 2)

    upper, lower = pl.ds(0, 16), pl.ds(16, 16)
    first = []
    z_copies = []
    for n, (to, d) in enumerate(((2, 3), (6, 5))):
        first.append(
            copy(hb.at[piece(d)], s1.at[n], x_s.at[0, n], x_r.at[0, n], at_z(to))
        )
    for n, (to, rows16) in enumerate(((2, upper), (6, lower))):
        first.append(
            copy(hb.at[(*piece(4), rows16)], s1h.at[n], x_s.at[1, n], x_r.at[1, n], at_z(to))
        )
    for n, (to, rows16) in enumerate(((2, lower), (6, upper))):
        z_copies.append(
            copy(hb.at[(*piece(to), rows16)], r2z.at[n, rows16], x_s.at[2, n], x_r.at[2, n], at_z(to))
        )
    for n, d in enumerate((1, 7)):
        first[n].wait()
        a, b = piece(d)
        m1[n] = (hown[a, b] + s1[n].astype(F32)).astype(BF16)
        z_copies.append(copy(m1.at[n], r1z.at[n], x_s.at[3, n], x_r.at[3, n], at_z(d)))
    for n, (d, rows16) in enumerate(((2, upper), (6, lower))):
        first[2 + n].wait()
        a, b = piece(d)
        m2[n] = (hown[a, b, rows16] + s1h[n].astype(F32)).astype(BF16)
        z_copies.append(
            copy(m2.at[n], r2z.at[n, rows16], x_s.at[4, n], x_r.at[4, n], at_z(d))
        )

    stage_b = []
    for c in stage_a[:3]:
        c.wait()
    total = pc[0, y] + qy[1].astype(F32) + qy[2].astype(F32) + qy[3].astype(F32)
    r0[...] = total
    r0b[...] = total.astype(BF16)
    for d in (2, 1, 3):
        src = r0b.at[lax.rem(x + d, 4)]
        stage_b.append(copy(src, fx.at[d], v_s.at[2, d], v_r.at[2, d], at_x(d)))
    for c in stage_a[3:]:
        c.wait()
    total = pc[1, x] + qx[1].astype(F32) + qx[2].astype(F32) + qx[3].astype(F32)
    r1[...] = total
    r1b[...] = total.astype(BF16)
    for d in (2, 1, 3):
        src = r1b.at[lax.rem(y + d, 4)]
        stage_b.append(copy(src, fy.at[d], v_s.at[3, d], v_r.at[3, d], at_y(d)))
    for c in stage_b:
        c.wait()

    def ordered(v):
        tiles = [v[:, 128 * i:128 * i + 128] for i in range(4)]
        tails = [v[:, 512 + 64 * i:576 + 64 * i] for i in range(4)]
        return jnp.concatenate([t for pair in zip(tiles, tails) for t in pair], axis=1)

    low = r0[x] + fx[1].astype(F32) + fx[2].astype(F32) + fx[3].astype(F32)
    high = r1[y] + fy[1].astype(F32) + fy[2].astype(F32) + fy[3].astype(F32)
    acc = jnp.concatenate([low, high], axis=0)
    held = hcap[...]
    clip_held = hclip[...]
    clip_unit = clip_held.astype(BF16).astype(F32)
    cap_unit = held.astype(BF16).astype(F32)
    pool_unit = pu[home, rows, :]
    grad = acc - 0.5 * clip_unit - 0.5 * pool_unit
    dcap_ref[...] = ordered(
        (grad - held * jnp.sum(held * grad, axis=1, keepdims=True)) / hlen[1]
    )

    for c in z_copies:
        c.wait()
    acc = hown[zl, zh] + r1z[0].astype(F32) + r1z[1].astype(F32)
    acc = acc + r2z[0].astype(F32) + r2z[1].astype(F32)
    grad = acc - 0.5 * cap_unit
    dclip_ref[...] = ordered(
        (grad - clip_held * jnp.sum(clip_held * grad, axis=1, keepdims=True)) / hlen[0]
    )


def body(clips, captions, video_id, logit_scale):
    vmem = pl.BlockSpec(memory_space=pltpu.VMEM)
    hbm = pl.BlockSpec(memory_space=pltpu.HBM)
    dma = lambda *shape: pltpu.SemaphoreType.DMA(shape)
    out = jax.ShapeDtypeStruct((32, 768), F32)
    V = pltpu.VMEM
    keep = lambda v: pltpu.with_memory_space_constraint(v, pltpu.HBM)
    d_clips, d_captions = pl.pallas_call(
        kernel,
        out_shape=(out, out),
        in_specs=[pl.BlockSpec(memory_space=pltpu.SMEM), hbm, hbm, hbm],
        out_specs=(vmem, vmem),
        scratch_shapes=[
            V((2, 192, 128), BF16), V((64, 128), jnp.int32),
            V((4, 48, 128), BF16), V((4, 48, 128), BF16), V((16, 192, 128), BF16),
            V((32, 768), F32), V((32, 768), F32), V((2, 32, 1), F32),
            V((768, 512), BF16), V((2, 4, 4, 16, 768), BF16),
            V((4, 128, 1), F32), V((1, 512), F32), V((1, 512), F32), V((4, 128, 1), F32),
            V((4, 128, 768), F32), V((4, 128, 1), F32), V((4, 1, 768), F32), V((4, 1, 768), F32),
            V((4, 128, 512), F32), V((4, 128, 512), F32), V((512, 512), F32), V((512, 512), F32),
            V((4, 128, 768), F32), V((4, 128), F32),
            V((4, 128), F32), V((16, 4, 128), F32), V((4, 128), F32), V((16, 4, 128), F32),
            V((2, 4, 32, 768), BF16), V((2, 4, 32, 768), BF16), V((2, 4, 32, 768), BF16),
            V((2, 4, 32, 768), F32), V((2, 32, 768), BF16), V((2, 16, 768), BF16),
            V((2, 32, 768), BF16), V((2, 16, 768), BF16), V((2, 32, 768), BF16),
            V((2, 32, 768), BF16),
            V((2, 4, 4, 16, 768), BF16), V((2, 4, 4, 16, 768), F32),
            V((4, 4, 16, 768), BF16), V((4, 4, 16, 768), BF16),
            V((4, 16, 768), F32), V((4, 16, 768), F32),
            V((4, 16, 768), BF16), V((4, 16, 768), BF16),
            V((4, 16, 768), BF16), V((4, 16, 768), BF16),
            dma(3), dma(4), dma(4), dma(8), dma(8), dma(8), dma(8), dma(2, 4), dma(2, 4),
            dma(2, 4, 4), dma(2, 4, 4),
            dma(4), dma(4), dma(2, 16), dma(2, 16), dma(1, 2), dma(1, 2), dma(5, 2), dma(5, 2),
            dma(4, 4), dma(4, 4),
        ],
        compiler_params=pltpu.CompilerParams(
            collective_id=0, has_side_effects=True, vmem_limit_bytes=48 * 1024 * 1024
        ),
        name="contrastive",
    )(logit_scale.reshape(1), keep(video_id.reshape(64, 128)), keep(clips.T), keep(captions.T))
    return logit_scale * d_clips, logit_scale * d_captions


def solution(mesh):
    in_specs = (P("dp", "mp"), P("dp", "mp"), P(), P())
    out_specs = (P(("dp", "mp"), None), P(("dp", "mp"), None))
    return jax.shard_map(body, mesh=mesh, in_specs=in_specs, out_specs=out_specs, check_vma=False)
```

```python
import jax
import jax.numpy as jnp
from jax import lax
from jax.experimental import pallas as pl
from jax.experimental.pallas import tpu as pltpu
from jax.sharding import PartitionSpec as P

EPSILON = 1e-06
NEGATIVE_FILL = -1e30
F32 = jnp.float32
BF16 = jnp.bfloat16
MESH = pl.DeviceIdType.MESH


def chip(x, y, z, core):
    return ((y * 2 + lax.rem(z, 2)) * 8 + x * 2 + core, lax.div(z, 2))


def kernel(
    scale_ref, vid_ref, clips_ref, caps_ref,
    dclip_ref, dcap_ref,
    raw, vid, pkt, ta, cr, hcap, hclip, hlen,
    clt, ct, vic, vjr, vir, vjc,
    pu, plen, eo, ei,
    ej, ek, ejt, ekt, pj, ctop,
    rst, rz, cst, cz,
    g, sb, hb, hown, s1, s1h, m1, m2, r1z, r2z,
    g2, pc, qy, qx, r0, r1, r0b, r1b, fx, fy,
    l_s, a2a_s, a2a_r, z_s, z_r, s_s, s_r, p_s, p_r, f_s, f_r, e_s, e_r,
    t_s, t_r, w_s, w_r, x_s, x_r, v_s, v_r,
):
    dp = lax.axis_index("dp")
    zh = lax.axis_index("mp")
    core = lax.rem(dp, 2)
    x = lax.rem(lax.div(dp, 2), 4)
    zl = lax.rem(lax.div(dp, 8), 2)
    y = lax.div(dp, 16)
    z = zh * 2 + zl
    home = zl * 2 + core
    sibling = chip(x, y, z, 1 - core)
    at_z = lambda d: chip(x, y, lax.rem(z + d, 8), core)
    at_x = lambda d: chip(lax.rem(x + d, 4), y, z, core)
    at_y = lambda d: chip(x, lax.rem(y + d, 4), z, core)

    others_z = (4, 3, 5, 2, 6, 1, 7)
    others_xy = sorted(
        [(i, j) for i in range(4) for j in range(4) if i or j],
        key=lambda t: -(min(t[0], 4 - t[0]) + min(t[1], 4 - t[1])),
    )
    at_xy = lambda i, j: chip(lax.rem(x + i, 4), lax.rem(y + j, 4), z, core)

    def copy(src, dst, send, recv, device):
        c = pltpu.make_async_remote_copy(
            src_ref=src, dst_ref=dst, send_sem=send, recv_sem=recv,
            device_id=device, device_id_type=MESH,
        )
        c.start()
        return c

    runs = [y * 8 + x, y * 8 + 4 + x]

    def owner(q):
        return chip(lax.rem(q, 4), lax.div(q, 8), z, core), lax.rem(lax.div(q, 4), 2)

    after = [owner(lax.rem(q + 1, 32)) for q in runs]
    before = [owner(lax.rem(q + 31, 32)) for q in runs]

    barrier = pltpu.get_barrier_semaphore()
    partners = [at_z(d) for d in others_z]
    partners += [chip(x, y, lax.rem(z + d, 8), 1 - core) for d in others_z]
    partners += [at_xy(i, j) for i, j in others_xy] + [sibling]
    for device in partners:
        pl.semaphore_signal(barrier, inc=1, device_id=device, device_id_type=MESH)
    loads = [
        pltpu.make_async_copy(src, dst, l_s.at[i])
        for i, (src, dst) in enumerate(((caps_ref, raw.at[1]), (clips_ref, raw.at[0]), (vid_ref, vid)))
    ]
    for c in loads:
        c.start()

    loads[0].wait()
    block = raw[1].astype(F32).T
    for k in range(4):
        pkt[k, 0:32] = block[32 * k:32 * k + 32, 0:128].astype(BF16)
        tail = block[32 * k:32 * k + 32, 128:192]
        pkt[k, 32:48] = jnp.concatenate([tail[0:16], tail[16:32]], axis=1).astype(BF16)
    ta[zh] = pkt[zh]
    loads[1].wait()
    slot = lambda at, c: lax.rem(at, 2) * 8 + c * 4 + lax.div(at, 2)
    mine = slot(z, core)
    cr[mine] = raw[0]

    loads[2].wait()
    sub = lax.broadcasted_iota(jnp.int32, (128, 128), 0)
    lane = lax.broadcasted_iota(jnp.int32, (128, 128), 1)
    eye = sub == lane

    def to_col(row):
        return jnp.sum(jnp.where(eye, row, 0.0), axis=1, keepdims=True)

    def to_row(col):
        return jnp.sum(jnp.where(eye, col, 0.0), axis=0, keepdims=True)

    def block_of(b):
        return (y * 2 + lax.div(b, 2)) * 8 + x * 2 + lax.rem(b, 2)

    def ids_of(row):
        return vid[pl.ds(row, 1), :].astype(F32)

    for b in range(4):
        ids = ids_of(block_of(b))
        vir[:, 128 * b:128 * b + 128] = ids
        vic[b] = to_col(ids)
    segment = lax.div(lax.broadcasted_iota(jnp.int32, (1, 128), 1), 16)
    for h in range(2):
        for grp in range(2):
            out = jnp.zeros((1, 128), F32)
            for s in range(8):
                a, b = grp * 2 + s // 4, s % 4
                ys, xs = (a, b) if h == 0 else (b, a)
                v = ids_of((ys * 2 + zl) * 8 + xs * 2 + core)
                shift = lax.rem(s * 16 + 256 - zh * 32 - h * 16, 128)
                out = jnp.where(segment == s, pltpu.roll(v, shift, 1), out)
            vjr[:, (h * 2 + grp) * 128:(h * 2 + grp + 1) * 128] = out
            vjc[h * 2 + grp] = to_col(out)

    pl.semaphore_wait(barrier, len(partners))

    pending = []
    for d in (2, 1, 3):
        to = lax.rem(zh + d, 4)
        pending.append(copy(pkt.at[to], ta.at[zh], a2a_s.at[d], a2a_r.at[d], (dp, to)))
    own = raw.at[0]
    sib_copies = [copy(own, cr.at[mine], s_s.at[0], s_r.at[0], sibling)]
    near = {d: copy(own, cr.at[mine], z_s.at[d], z_r.at[d], at_z(d)) for d in (1, 7, 2, 6)}

    def to_sibling(d):
        ref = cr.at[slot(lax.rem(z + 8 - d, 8), core)]
        sib_copies.append(copy(ref, ref, s_s.at[d], s_r.at[d], sibling))

    far = {}

    def relay(d, to, sem, rows):
        near[d].wait()
        at = slot(lax.rem(z + 8 - d, 8), core)
        ref = cr.at[at] if rows is None else cr.at[at, pl.ds(rows, 96)]
        far[sem] = copy(ref, ref, z_s.at[sem], z_r.at[sem], at_z(to))
        to_sibling(d)


    def unpacked(parts):
        low = lax.broadcasted_iota(jnp.int32, (16, 128), 1) < 64
        tiles = [p[0:32].astype(F32) for p in parts]
        tails = [p[32:48].astype(F32) for p in parts]
        for i in (0, 2):
            left, right = tails[i], tails[i + 1]
            upper = jnp.where(low, left, pltpu.roll(right, 64, 1))
            lower = jnp.where(low, pltpu.roll(left, 64, 1), right)
            tiles.append(jnp.concatenate([upper, lower], axis=0))
        return jnp.concatenate(tiles, axis=1)

    def lengths(full):
        return jnp.sqrt(jnp.sum(full * full, axis=1, keepdims=True) + EPSILON)

    for c in pending:
        c.wait()
    full = unpacked([ta[k] for k in range(4)])
    length = lengths(full)
    full = full / length
    hcap[...] = full
    hlen[1] = length
    u = full.astype(BF16)
    ct[0, y, x] = u[0:16]
    ct[1, x, y] = u[16:32]
    axes = ((at_x, at_y, y, x), (at_y, at_x, x, y))
    stage_a = [[], []]
    for d in (2, 1, 3):
        for h, (along, _, i, j) in enumerate(axes):
            ref = ct.at[h, i, j]
            stage_a[h].append((d, copy(ref, ref, p_s.at[h, d], p_r.at[h, d], along(d))))
    stage_b = []

    def forward(h, e):
        _, across, i, j = axes[h]
        ref = ct.at[h, i, lax.rem(j + 4 - e, 4)]
        for d in (2, 1, 3):
            stage_b.append(copy(ref, ref, f_s.at[h, e, d], f_r.at[h, e, d], across(d)))

    relay(1, 2, 3, None)
    relay(7, 6, 5, None)
    relay(2, 2, 4, 0)
    relay(6, 6, 0, 96)
    forward(0, 0)
    forward(1, 0)
    for n in (1, 2, 0):
        for h in range(2):
            d, c = stage_a[h][n]
            c.wait()
            forward(h, d)
    for d in (3, 5):
        far[d].wait()
        to_sibling(d)
    far[4].wait()
    far[0].wait()
    to_sibling(4)
    for c in sib_copies:
        c.wait()

    def normalise(b, carry):
        parts = [cr[4 * b + k].astype(F32) for k in range(4)]
        total = sum(jnp.sum(p * p, axis=0, keepdims=True) for p in parts)
        inverse = 1.0 / jnp.sqrt(total + EPSILON)
        columns = pl.ds(pl.multiple_of(128 * b, 128), 128)
        for k, p in enumerate(parts):
            p = (p * inverse).astype(BF16)
            clt[128 * k:128 * k + 128, columns] = p[0:128]
            clt[512 + 64 * k:576 + 64 * k, columns] = p[128:192]
        return carry

    lax.fori_loop(0, 4, normalise, 0)

    edge_copies = []
    for r in range(2):
        ids = vir[:, 256 * r:256 * r + 256]
        col = jnp.concatenate([vic[2 * r], vic[2 * r + 1]], axis=0)
        alike = jnp.where(col == ids, 1.0, 0.0).astype(BF16)
        local = lax.dot_general(
            alike, clt[:, 256 * r:256 * r + 256], (((1,), (1,)), ((), ())),
            preferred_element_type=F32,
        )
        pu[2 * r] = local[0:128]
        pu[2 * r + 1] = local[128:256]
        eo[2 * r] = local[0:1]
        eo[2 * r + 1] = local[255:256]
        device, side = before[r]
        edge_copies.append(
            copy(eo.at[2 * r], ei.at[side * 2 + 1], e_s.at[2 * r], e_r.at[side * 2 + 1], device)
        )
        device, side = after[r]
        edge_copies.append(
            copy(eo.at[2 * r + 1], ei.at[side * 2], e_s.at[2 * r + 1], e_r.at[side * 2], device)
        )
    for c in stage_b:
        c.wait()

    scale = scale_ref[0]
    ej[...] = jnp.dot(
        ct[...].reshape(512, 768), clt[...], preferred_element_type=F32
    ).reshape(4, 128, 512)
    column = lax.broadcasted_iota(jnp.int32, (1, 512), 1)
    clip_pos = (y * 2 + lax.div(column, 256)) * 1024 + x * 256 + lax.rem(column, 256)

    def pass_one(b, top):
        j = b * 128 + lax.broadcasted_iota(jnp.int32, (128, 1), 0)
        half = lax.div(j, 256)
        first = lax.rem(lax.div(j, 64), 4)
        second = lax.rem(lax.div(j, 16), 4)
        ypos = jnp.where(half == 0, first, second)
        xpos = jnp.where(half == 0, second, first)
        cap_pos = ((ypos * 2 + zl) * 8 + xpos * 2 + core) * 128 + zh * 32 + half * 16 + lax.rem(j, 16)
        alike = vjc[b] == vir[...]
        allowed = jnp.logical_not(alike) | (cap_pos == clip_pos)
        s = jnp.where(allowed, scale * ej[b], NEGATIVE_FILL)
        ek[b] = s
        high = jnp.max(s, axis=1, keepdims=True)
        e = jnp.exp(s - high)
        ej[b] = e
        high = to_row(high)
        ctop[pl.ds(b, 1), :] = high
        cst[pl.ds(b, 1), :] = high + jnp.log(to_row(jnp.sum(e, axis=1, keepdims=True)))
        return jnp.maximum(top, jnp.max(s, axis=0, keepdims=True))

    clip_top = lax.fori_loop(0, 4, pass_one, jnp.full((1, 512), NEGATIVE_FILL, F32))
    stats = []
    for i, j in others_xy:
        n = i * 4 + j
        stats.append(copy(cst, cz.at[n], t_s.at[1, n], t_r.at[1, n], at_xy(i, j)))

    def pass_two(b, total):
        e = jnp.exp(ek[b] - clip_top)
        ek[b] = e
        return total + jnp.sum(e, axis=0, keepdims=True)

    clip_lse = clip_top + jnp.log(lax.fori_loop(0, 4, pass_two, jnp.zeros((1, 512), F32)))
    for b in range(4):
        rst[b:b + 1, :] = clip_lse[:, b * 128:(b + 1) * 128]
    for d in others_z + (0,):
        for i in range(2):
            if d or i:
                n = i * 8 + d
                device = chip(x, y, lax.rem(z + d, 8), core if i == 0 else 1 - core)
                stats.append(copy(rst, rz.at[n], t_s.at[0, n], t_r.at[0, n], device))
    rz[0] = rst[...]
    cz[0] = cst[...]

    def joined(ref):
        values = ref[...]
        top = jnp.max(values, axis=0)
        return top + jnp.log(jnp.sum(jnp.exp(values - top), axis=0))

    for b in range(4):
        ejt[:, b * 128:(b + 1) * 128] = ej[b].T
        ekt[:, b * 128:(b + 1) * 128] = ek[b].T
    parts = [cr[4 * home + k].astype(F32) for k in range(4)]
    full = jnp.concatenate([p[0:128] for p in parts] + [p[128:192] for p in parts], axis=0)
    pj[0] = full.T
    rows = pl.ds(pl.multiple_of(zh * 32, 32), 32)
    full = pj[0, rows, :]
    length = lengths(full)
    hclip[...] = full / length
    hlen[0] = length
    for c in edge_copies:
        c.wait()
    for b in range(4):
        r = b // 2
        q = runs[r]
        left = ids_of(jnp.maximum(2 * q - 1, 0))[:, 127:128]
        right = ids_of(jnp.minimum(2 * q + 2, 63))[:, 0:1]
        from_left = jnp.where(vic[b] == left, jnp.where(q > 0, 1.0, 0.0), 0.0)
        from_right = jnp.where(vic[b] == right, jnp.where(q < 31, 1.0, 0.0), 0.0)
        pooled = pu[b] + from_left * ei[2 * r] + from_right * ei[2 * r + 1]
        length = lengths(pooled)
        plen[b] = length
        pu[b] = pooled * (1.0 / length)

    def projected(b, carry):
        alike = jnp.where(vic[b] == vjr[...], 1.0, 0.0).astype(BF16)
        acc = jnp.dot(alike, ct[...].reshape(512, 768), preferred_element_type=F32)
        pool = pu[b]
        acc = acc - pool * jnp.sum(pool * acc, axis=1, keepdims=True)
        pj[b] = acc * (0.5 / plen[b])
        return carry

    lax.fori_loop(0, 4, projected, 0)

    for c in stats:
        c.wait()
    whole = joined(rz)
    whole = jnp.concatenate([whole[b:b + 1] for b in range(4)], axis=1)
    clip_line = 0.5 * jnp.exp(clip_top - whole)
    for b in range(4):
        rst[b:b + 1, :] = clip_line[:, b * 128:(b + 1) * 128]
    cap_fac = 0.5 * jnp.exp(ctop[...] - joined(cz))
    cap_line = jnp.concatenate([cap_fac[b:b + 1] for b in range(4)], axis=1)

    def weigh(c):
        blocks = [c, 2 + c]
        w = []
        for b in blocks:
            rows = pl.ds(pl.multiple_of(128 * b, 128), 128)
            w.append(
                (ekt[rows, :] * to_col(rst[pl.ds(b, 1), :]) + ejt[rows, :] * cap_line).astype(BF16)
            )
        part = jnp.dot(
            jnp.concatenate(w, axis=0), ct[...].reshape(512, 768), preferred_element_type=F32
        )
        return [part[128 * i:128 * i + 128] - pj[b] for i, b in enumerate(blocks)]

    sib_copies = []
    for r, part in enumerate(weigh(1 - core)):
        g[r] = part.astype(BF16).reshape(4, 32, 768)
        sib_copies.append(copy(g.at[r], sb.at[r], w_s.at[0, r], w_r.at[0, r], sibling))

    stage_a = []

    w = [
        (ek[b] * clip_line + ej[b] * to_col(cap_fac[b:b + 1])).astype(BF16) for b in range(4)
    ]
    both_halves = lax.dot_general(
        jnp.concatenate(w, axis=0), clt[...], (((1,), (1,)), ((), ())),
        preferred_element_type=F32,
    ).reshape(2, 4, 4, 16, 768)

    def caption_part(h):
        part = both_halves[h]
        pc[h] = part
        g2[h] = part.astype(BF16)
        at, to, first = ((at_y, qy, y), (at_x, qx, x))[h]
        for d in (2, 1, 3):
            src = g2.at[h, lax.rem(first + d, 4)]
            stage_a.append(copy(src, to.at[d], v_s.at[h, d], v_r.at[h, d], at(d)))

    caption_part(0)
    caption_part(1)
    for r, part in enumerate(weigh(core)):
        hown[r] = part.reshape(4, 32, 768)

    for c in sib_copies:
        c.wait()
    for r in range(2):
        both = hown[r] + sb[r].astype(F32)
        hown[r] = both
        hb[r] = both.astype(BF16)

    def piece(d):
        to = lax.rem(z + d, 8)
        return lax.rem(to, 2), lax.div(to, 2)

    upper, lower = pl.ds(0, 16), pl.ds(16, 16)
    first = []
    z_copies = []
    for n, (to, d) in enumerate(((2, 3), (6, 5))):
        first.append(
            copy(hb.at[piece(d)], s1.at[n], x_s.at[0, n], x_r.at[0, n], at_z(to))
        )
    for n, (to, rows16) in enumerate(((2, upper), (6, lower))):
        first.append(
            copy(hb.at[(*piece(4), rows16)], s1h.at[n], x_s.at[1, n], x_r.at[1, n], at_z(to))
        )
    for n, (to, rows16) in enumerate(((2, lower), (6, upper))):
        z_copies.append(
            copy(hb.at[(*piece(to), rows16)], r2z.at[n, rows16], x_s.at[2, n], x_r.at[2, n], at_z(to))
        )
    for n, d in enumerate((1, 7)):
        first[n].wait()
        a, b = piece(d)
        m1[n] = (hown[a, b] + s1[n].astype(F32)).astype(BF16)
        z_copies.append(copy(m1.at[n], r1z.at[n], x_s.at[3, n], x_r.at[3, n], at_z(d)))
    for n, (d, rows16) in enumerate(((2, upper), (6, lower))):
        first[2 + n].wait()
        a, b = piece(d)
        m2[n] = (hown[a, b, rows16] + s1h[n].astype(F32)).astype(BF16)
        z_copies.append(
            copy(m2.at[n], r2z.at[n, rows16], x_s.at[4, n], x_r.at[4, n], at_z(d))
        )

    stage_b = []
    for c in stage_a[:3]:
        c.wait()
    total = pc[0, y] + qy[1].astype(F32) + qy[2].astype(F32) + qy[3].astype(F32)
    r0[...] = total
    r0b[...] = total.astype(BF16)
    for d in (2, 1, 3):
        src = r0b.at[lax.rem(x + d, 4)]
        stage_b.append(copy(src, fx.at[d], v_s.at[2, d], v_r.at[2, d], at_x(d)))
    for c in stage_a[3:]:
        c.wait()
    total = pc[1, x] + qx[1].astype(F32) + qx[2].astype(F32) + qx[3].astype(F32)
    r1[...] = total
    r1b[...] = total.astype(BF16)
    for d in (2, 1, 3):
        src = r1b.at[lax.rem(y + d, 4)]
        stage_b.append(copy(src, fy.at[d], v_s.at[3, d], v_r.at[3, d], at_y(d)))
    for c in stage_b:
        c.wait()

    def ordered(v):
        tiles = [v[:, 128 * i:128 * i + 128] for i in range(4)]
        tails = [v[:, 512 + 64 * i:576 + 64 * i] for i in range(4)]
        return jnp.concatenate([t for pair in zip(tiles, tails) for t in pair], axis=1)

    low = r0[x] + fx[1].astype(F32) + fx[2].astype(F32) + fx[3].astype(F32)
    high = r1[y] + fy[1].astype(F32) + fy[2].astype(F32) + fy[3].astype(F32)
    acc = jnp.concatenate([low, high], axis=0)
    held = hcap[...]
    clip_held = hclip[...]
    clip_unit = clip_held.astype(BF16).astype(F32)
    cap_unit = held.astype(BF16).astype(F32)
    pool_unit = pu[home, rows, :]
    grad = acc - 0.5 * clip_unit - 0.5 * pool_unit
    dcap_ref[...] = ordered(
        (grad - held * jnp.sum(held * grad, axis=1, keepdims=True)) / hlen[1]
    )

    for c in z_copies:
        c.wait()
    acc = hown[zl, zh] + r1z[0].astype(F32) + r1z[1].astype(F32)
    acc = acc + r2z[0].astype(F32) + r2z[1].astype(F32)
    grad = acc - 0.5 * cap_unit
    dclip_ref[...] = ordered(
        (grad - clip_held * jnp.sum(clip_held * grad, axis=1, keepdims=True)) / hlen[0]
    )


def body(clips, captions, video_id, logit_scale):
    vmem = pl.BlockSpec(memory_space=pltpu.VMEM)
    hbm = pl.BlockSpec(memory_space=pltpu.HBM)
    dma = lambda *shape: pltpu.SemaphoreType.DMA(shape)
    out = jax.ShapeDtypeStruct((32, 768), F32)
    V = pltpu.VMEM
    keep = lambda v: pltpu.with_memory_space_constraint(v, pltpu.HBM)
    d_clips, d_captions = pl.pallas_call(
        kernel,
        out_shape=(out, out),
        in_specs=[pl.BlockSpec(memory_space=pltpu.SMEM), hbm, hbm, hbm],
        out_specs=(vmem, vmem),
        scratch_shapes=[
            V((2, 192, 128), BF16), V((64, 128), jnp.int32),
            V((4, 48, 128), BF16), V((4, 48, 128), BF16), V((16, 192, 128), BF16),
            V((32, 768), F32), V((32, 768), F32), V((2, 32, 1), F32),
            V((768, 512), BF16), V((2, 4, 4, 16, 768), BF16),
            V((4, 128, 1), F32), V((1, 512), F32), V((1, 512), F32), V((4, 128, 1), F32),
            V((4, 128, 768), F32), V((4, 128, 1), F32), V((4, 1, 768), F32), V((4, 1, 768), F32),
            V((4, 128, 512), F32), V((4, 128, 512), F32), V((512, 512), F32), V((512, 512), F32),
            V((4, 128, 768), F32), V((4, 128), F32),
            V((4, 128), F32), V((16, 4, 128), F32), V((4, 128), F32), V((16, 4, 128), F32),
            V((2, 4, 32, 768), BF16), V((2, 4, 32, 768), BF16), V((2, 4, 32, 768), BF16),
            V((2, 4, 32, 768), F32), V((2, 32, 768), BF16), V((2, 16, 768), BF16),
            V((2, 32, 768), BF16), V((2, 16, 768), BF16), V((2, 32, 768), BF16),
            V((2, 32, 768), BF16),
            V((2, 4, 4, 16, 768), BF16), V((2, 4, 4, 16, 768), F32),
            V((4, 4, 16, 768), BF16), V((4, 4, 16, 768), BF16),
            V((4, 16, 768), F32), V((4, 16, 768), F32),
            V((4, 16, 768), BF16), V((4, 16, 768), BF16),
            V((4, 16, 768), BF16), V((4, 16, 768), BF16),
            dma(3), dma(4), dma(4), dma(8), dma(8), dma(8), dma(8), dma(2, 4), dma(2, 4),
            dma(2, 4, 4), dma(2, 4, 4),
            dma(4), dma(4), dma(2, 16), dma(2, 16), dma(1, 2), dma(1, 2), dma(5, 2), dma(5, 2),
            dma(4, 4), dma(4, 4),
        ],
        compiler_params=pltpu.CompilerParams(
            collective_id=0, has_side_effects=True, vmem_limit_bytes=48 * 1024 * 1024
        ),
        name="contrastive",
    )(logit_scale.reshape(1), keep(video_id.reshape(64, 128)), keep(clips.T), keep(captions.T))
    return logit_scale * d_clips, logit_scale * d_captions


def solution(mesh):
    in_specs = (P("dp", "mp"), P("dp", "mp"), P(), P())
    out_specs = (P(("dp", "mp"), None), P(("dp", "mp"), None))
    return jax.shard_map(body, mesh=mesh, in_specs=in_specs, out_specs=out_specs, check_vma=False)
```

```python
import jax
import jax.numpy as jnp
from jax import lax
from jax.experimental import pallas as pl
from jax.experimental.pallas import tpu as pltpu
from jax.sharding import PartitionSpec as P

EPSILON = 1e-06
NEGATIVE_FILL = -1e30
F32 = jnp.float32
BF16 = jnp.bfloat16
MESH = pl.DeviceIdType.MESH


def chip(x, y, z, core):
    return ((y * 2 + lax.rem(z, 2)) * 8 + x * 2 + core, lax.div(z, 2))


def kernel(
    scale_ref, vid_ref, clips_ref, caps_ref,
    dclip_ref, dcap_ref,
    raw, vid, pkt, ta, cr, hcap, hclip, hlen,
    clt, ct, vic, vjr, vir, vjc,
    pu, plen, eo, ei,
    ej, ek, ejt, ekt, pj, ctop,
    rst, rz, cst, cz,
    g, sb, hb, hown, s1, s1h, m1, m2, r1z, r2z,
    g2, qy, qx, r0, r1, r0b, r1b, fx, fy,
    l_s, a2a_s, a2a_r, z_s, z_r, s_s, s_r, p_s, p_r, f_s, f_r, e_s, e_r,
    t_s, t_r, w_s, w_r, x_s, x_r, v_s, v_r,
):
    dp = lax.axis_index("dp")
    zh = lax.axis_index("mp")
    core = lax.rem(dp, 2)
    x = lax.rem(lax.div(dp, 2), 4)
    zl = lax.rem(lax.div(dp, 8), 2)
    y = lax.div(dp, 16)
    z = zh * 2 + zl
    home = zl * 2 + core
    sibling = chip(x, y, z, 1 - core)
    at_z = lambda d: chip(x, y, lax.rem(z + d, 8), core)
    at_x = lambda d: chip(lax.rem(x + d, 4), y, z, core)
    at_y = lambda d: chip(x, lax.rem(y + d, 4), z, core)

    others_z = (4, 3, 5, 2, 6, 1, 7)
    others_xy = sorted(
        [(i, j) for i in range(4) for j in range(4) if i or j],
        key=lambda t: -(min(t[0], 4 - t[0]) + min(t[1], 4 - t[1])),
    )
    at_xy = lambda i, j: chip(lax.rem(x + i, 4), lax.rem(y + j, 4), z, core)

    def copy(src, dst, send, recv, device):
        c = pltpu.make_async_remote_copy(
            src_ref=src, dst_ref=dst, send_sem=send, recv_sem=recv,
            device_id=device, device_id_type=MESH,
        )
        c.start()
        return c

    runs = [y * 8 + x, y * 8 + 4 + x]

    def owner(q):
        return chip(lax.rem(q, 4), lax.div(q, 8), z, core), lax.rem(lax.div(q, 4), 2)

    after = [owner(lax.rem(q + 1, 32)) for q in runs]
    before = [owner(lax.rem(q + 31, 32)) for q in runs]

    barrier = pltpu.get_barrier_semaphore()
    partners = [at_z(d) for d in others_z]
    partners += [chip(x, y, lax.rem(z + d, 8), 1 - core) for d in others_z]
    partners += [at_xy(i, j) for i, j in others_xy] + [sibling]
    for device in partners:
        pl.semaphore_signal(barrier, inc=1, device_id=device, device_id_type=MESH)
    loads = [
        pltpu.make_async_copy(src, dst, l_s.at[i])
        for i, (src, dst) in enumerate(((caps_ref, raw.at[1]), (clips_ref, raw.at[0]), (vid_ref, vid)))
    ]
    for c in loads:
        c.start()

    loads[0].wait()
    block = raw[1].astype(F32).T
    for k in range(4):
        pkt[k, 0:32] = block[32 * k:32 * k + 32, 0:128].astype(BF16)
        tail = block[32 * k:32 * k + 32, 128:192]
        pkt[k, 32:48] = jnp.concatenate([tail[0:16], tail[16:32]], axis=1).astype(BF16)
    ta[zh] = pkt[zh]
    loads[1].wait()
    slot = lambda at, c: lax.rem(at, 2) * 8 + c * 4 + lax.div(at, 2)
    mine = slot(z, core)
    cr[mine] = raw[0]

    loads[2].wait()
    sub = lax.broadcasted_iota(jnp.int32, (128, 128), 0)
    lane = lax.broadcasted_iota(jnp.int32, (128, 128), 1)
    eye = sub == lane

    def to_col(row):
        return jnp.sum(jnp.where(eye, row, 0.0), axis=1, keepdims=True)

    def to_row(col):
        return jnp.sum(jnp.where(eye, col, 0.0), axis=0, keepdims=True)

    def block_of(b):
        return (y * 2 + lax.div(b, 2)) * 8 + x * 2 + lax.rem(b, 2)

    def ids_of(row):
        return vid[pl.ds(row, 1), :].astype(F32)

    for b in range(4):
        ids = ids_of(block_of(b))
        vir[:, 128 * b:128 * b + 128] = ids
        vic[b] = to_col(ids)
    segment = lax.div(lax.broadcasted_iota(jnp.int32, (1, 128), 1), 16)
    for h in range(2):
        for grp in range(2):
            out = jnp.zeros((1, 128), F32)
            for s in range(8):
                a, b = grp * 2 + s // 4, s % 4
                ys, xs = (a, b) if h == 0 else (b, a)
                v = ids_of((ys * 2 + zl) * 8 + xs * 2 + core)
                shift = lax.rem(s * 16 + 256 - zh * 32 - h * 16, 128)
                out = jnp.where(segment == s, pltpu.roll(v, shift, 1), out)
            vjr[:, (h * 2 + grp) * 128:(h * 2 + grp + 1) * 128] = out
            vjc[h * 2 + grp] = to_col(out)

    pl.semaphore_wait(barrier, len(partners))

    pending = []
    for d in (2, 1, 3):
        to = lax.rem(zh + d, 4)
        pending.append(copy(pkt.at[to], ta.at[zh], a2a_s.at[d], a2a_r.at[d], (dp, to)))
    own = raw.at[0]
    sib_copies = [copy(own, cr.at[mine], s_s.at[0], s_r.at[0], sibling)]
    near = {d: copy(own, cr.at[mine], z_s.at[d], z_r.at[d], at_z(d)) for d in (1, 7, 2, 6)}

    def to_sibling(d):
        ref = cr.at[slot(lax.rem(z + 8 - d, 8), core)]
        sib_copies.append(copy(ref, ref, s_s.at[d], s_r.at[d], sibling))

    far = {}

    def relay(d, to, sem, rows):
        near[d].wait()
        at = slot(lax.rem(z + 8 - d, 8), core)
        ref = cr.at[at] if rows is None else cr.at[at, pl.ds(rows, 96)]
        far[sem] = copy(ref, ref, z_s.at[sem], z_r.at[sem], at_z(to))
        to_sibling(d)


    def unpacked(parts):
        low = lax.broadcasted_iota(jnp.int32, (16, 128), 1) < 64
        tiles = [p[0:32].astype(F32) for p in parts]
        tails = [p[32:48].astype(F32) for p in parts]
        for i in (0, 2):
            left, right = tails[i], tails[i + 1]
            upper = jnp.where(low, left, pltpu.roll(right, 64, 1))
            lower = jnp.where(low, pltpu.roll(left, 64, 1), right)
            tiles.append(jnp.concatenate([upper, lower], axis=0))
        return jnp.concatenate(tiles, axis=1)

    def lengths(full):
        return jnp.sqrt(jnp.sum(full * full, axis=1, keepdims=True) + EPSILON)

    for c in pending:
        c.wait()
    full = unpacked([ta[k] for k in range(4)])
    length = lengths(full)
    full = full / length
    hcap[...] = full
    hlen[1] = length
    u = full.astype(BF16)
    ct[0, y, x] = u[0:16]
    ct[1, x, y] = u[16:32]
    axes = ((at_x, at_y, y, x), (at_y, at_x, x, y))
    stage_a = [[], []]
    for d in (2, 1, 3):
        for h, (along, _, i, j) in enumerate(axes):
            ref = ct.at[h, i, j]
            stage_a[h].append((d, copy(ref, ref, p_s.at[h, d], p_r.at[h, d], along(d))))
    stage_b = []

    def forward(h, e):
        _, across, i, j = axes[h]
        ref = ct.at[h, i, lax.rem(j + 4 - e, 4)]
        for d in (2, 1, 3):
            stage_b.append(copy(ref, ref, f_s.at[h, e, d], f_r.at[h, e, d], across(d)))

    relay(1, 2, 3, None)
    relay(7, 6, 5, None)
    relay(2, 2, 4, 0)
    relay(6, 6, 0, 96)
    forward(0, 0)
    forward(1, 0)
    for n in (1, 2, 0):
        for h in range(2):
            d, c = stage_a[h][n]
            c.wait()
            forward(h, d)
    for d in (3, 5):
        far[d].wait()
        to_sibling(d)
    far[4].wait()
    far[0].wait()
    to_sibling(4)
    for c in sib_copies:
        c.wait()

    def normalise(b, carry):
        parts = [cr[4 * b + k].astype(F32) for k in range(4)]
        total = sum(jnp.sum(p * p, axis=0, keepdims=True) for p in parts)
        inverse = 1.0 / jnp.sqrt(total + EPSILON)
        columns = pl.ds(pl.multiple_of(128 * b, 128), 128)
        for k, p in enumerate(parts):
            p = (p * inverse).astype(BF16)
            clt[128 * k:128 * k + 128, columns] = p[0:128]
            clt[512 + 64 * k:576 + 64 * k, columns] = p[128:192]
        return carry

    lax.fori_loop(0, 4, normalise, 0)

    edge_copies = []
    for r in range(2):
        ids = vir[:, 256 * r:256 * r + 256]
        col = jnp.concatenate([vic[2 * r], vic[2 * r + 1]], axis=0)
        alike = jnp.where(col == ids, 1.0, 0.0).astype(BF16)
        local = lax.dot_general(
            alike, clt[:, 256 * r:256 * r + 256], (((1,), (1,)), ((), ())),
            preferred_element_type=F32,
        )
        pu[2 * r] = local[0:128]
        pu[2 * r + 1] = local[128:256]
        eo[2 * r] = local[0:1]
        eo[2 * r + 1] = local[255:256]
        device, side = before[r]
        edge_copies.append(
            copy(eo.at[2 * r], ei.at[side * 2 + 1], e_s.at[2 * r], e_r.at[side * 2 + 1], device)
        )
        device, side = after[r]
        edge_copies.append(
            copy(eo.at[2 * r + 1], ei.at[side * 2], e_s.at[2 * r + 1], e_r.at[side * 2], device)
        )
    for c in stage_b:
        c.wait()

    scale = scale_ref[0]
    ej[...] = jnp.dot(
        ct[...].reshape(512, 768), clt[...], preferred_element_type=F32
    ).reshape(4, 128, 512)
    column = lax.broadcasted_iota(jnp.int32, (1, 512), 1)
    clip_pos = (y * 2 + lax.div(column, 256)) * 1024 + x * 256 + lax.rem(column, 256)

    def pass_one(b, top):
        j = b * 128 + lax.broadcasted_iota(jnp.int32, (128, 1), 0)
        half = lax.div(j, 256)
        first = lax.rem(lax.div(j, 64), 4)
        second = lax.rem(lax.div(j, 16), 4)
        ypos = jnp.where(half == 0, first, second)
        xpos = jnp.where(half == 0, second, first)
        cap_pos = ((ypos * 2 + zl) * 8 + xpos * 2 + core) * 128 + zh * 32 + half * 16 + lax.rem(j, 16)
        alike = vjc[b] == vir[...]
        allowed = jnp.logical_not(alike) | (cap_pos == clip_pos)
        s = jnp.where(allowed, scale * ej[b], NEGATIVE_FILL)
        ek[b] = s
        high = jnp.max(s, axis=1, keepdims=True)
        e = jnp.exp(s - high)
        ej[b] = e
        high = to_row(high)
        ctop[pl.ds(b, 1), :] = high
        cst[pl.ds(b, 1), :] = high + jnp.log(to_row(jnp.sum(e, axis=1, keepdims=True)))
        return jnp.maximum(top, jnp.max(s, axis=0, keepdims=True))

    clip_top = lax.fori_loop(0, 4, pass_one, jnp.full((1, 512), NEGATIVE_FILL, F32))
    stats = []
    for i, j in others_xy:
        n = i * 4 + j
        stats.append(copy(cst, cz.at[n], t_s.at[1, n], t_r.at[1, n], at_xy(i, j)))

    def pass_two(b, total):
        e = jnp.exp(ek[b] - clip_top)
        ek[b] = e
        return total + jnp.sum(e, axis=0, keepdims=True)

    clip_lse = clip_top + jnp.log(lax.fori_loop(0, 4, pass_two, jnp.zeros((1, 512), F32)))
    for b in range(4):
        rst[b:b + 1, :] = clip_lse[:, b * 128:(b + 1) * 128]
    for d in others_z + (0,):
        for i in range(2):
            if d or i:
                n = i * 8 + d
                device = chip(x, y, lax.rem(z + d, 8), core if i == 0 else 1 - core)
                stats.append(copy(rst, rz.at[n], t_s.at[0, n], t_r.at[0, n], device))
    rz[0] = rst[...]
    cz[0] = cst[...]

    def joined(ref):
        values = ref[...]
        top = jnp.max(values, axis=0)
        return top + jnp.log(jnp.sum(jnp.exp(values - top), axis=0))

    for b in range(4):
        ejt[:, b * 128:(b + 1) * 128] = ej[b].T
        ekt[:, b * 128:(b + 1) * 128] = ek[b].T
    parts = [cr[4 * home + k].astype(F32) for k in range(4)]
    full = jnp.concatenate([p[0:128] for p in parts] + [p[128:192] for p in parts], axis=0)
    pj[0] = full.T
    rows = pl.ds(pl.multiple_of(zh * 32, 32), 32)
    full = pj[0, rows, :]
    length = lengths(full)
    hclip[...] = full / length
    hlen[0] = length
    for c in edge_copies:
        c.wait()
    for b in range(4):
        r = b // 2
        q = runs[r]
        left = ids_of(jnp.maximum(2 * q - 1, 0))[:, 127:128]
        right = ids_of(jnp.minimum(2 * q + 2, 63))[:, 0:1]
        from_left = jnp.where(vic[b] == left, jnp.where(q > 0, 1.0, 0.0), 0.0)
        from_right = jnp.where(vic[b] == right, jnp.where(q < 31, 1.0, 0.0), 0.0)
        pooled = pu[b] + from_left * ei[2 * r] + from_right * ei[2 * r + 1]
        length = lengths(pooled)
        plen[b] = length
        pu[b] = pooled * (1.0 / length)

    def projected(b, carry):
        alike = jnp.where(vic[b] == vjr[...], 1.0, 0.0).astype(BF16)
        acc = jnp.dot(alike, ct[...].reshape(512, 768), preferred_element_type=F32)
        pool = pu[b]
        acc = acc - pool * jnp.sum(pool * acc, axis=1, keepdims=True)
        pj[b] = acc * (0.5 / plen[b])
        return carry

    lax.fori_loop(0, 4, projected, 0)

    for c in stats:
        c.wait()
    whole = joined(rz)
    whole = jnp.concatenate([whole[b:b + 1] for b in range(4)], axis=1)
    clip_line = 0.5 * jnp.exp(clip_top - whole)
    for b in range(4):
        rst[b:b + 1, :] = clip_line[:, b * 128:(b + 1) * 128]
    cap_fac = 0.5 * jnp.exp(ctop[...] - joined(cz))
    cap_line = jnp.concatenate([cap_fac[b:b + 1] for b in range(4)], axis=1)

    def weigh(c):
        blocks = [c, 2 + c]
        w = []
        for b in blocks:
            rows = pl.ds(pl.multiple_of(128 * b, 128), 128)
            w.append(
                (ekt[rows, :] * to_col(rst[pl.ds(b, 1), :]) + ejt[rows, :] * cap_line).astype(BF16)
            )
        part = jnp.dot(
            jnp.concatenate(w, axis=0), ct[...].reshape(512, 768), preferred_element_type=F32
        )
        return [part[128 * i:128 * i + 128] - pj[b] for i, b in enumerate(blocks)]

    sib_copies = []
    for r, part in enumerate(weigh(1 - core)):
        g[r] = part.astype(BF16).reshape(4, 32, 768)
        sib_copies.append(copy(g.at[r], sb.at[r], w_s.at[0, r], w_r.at[0, r], sibling))

    stage_a = []

    w = [
        (ek[b] * clip_line + ej[b] * to_col(cap_fac[b:b + 1])).astype(BF16) for b in range(4)
    ]
    both_halves = lax.dot_general(
        jnp.concatenate(w, axis=0), clt[...], (((1,), (1,)), ((), ())),
        preferred_element_type=F32,
    ).reshape(2, 4, 4, 16, 768)

    def caption_part(h):
        part = both_halves[h]
        g2[h] = part.astype(BF16)
        at, to, first = ((at_y, qy, y), (at_x, qx, x))[h]
        for d in (2, 1, 3):
            src = g2.at[h, lax.rem(first + d, 4)]
            stage_a.append(copy(src, to.at[d], v_s.at[h, d], v_r.at[h, d], at(d)))

    caption_part(0)
    caption_part(1)
    for r, part in enumerate(weigh(core)):
        hown[r] = part.reshape(4, 32, 768)

    for c in sib_copies:
        c.wait()
    for r in range(2):
        both = hown[r] + sb[r].astype(F32)
        hown[r] = both
        hb[r] = both.astype(BF16)

    def piece(d):
        to = lax.rem(z + d, 8)
        return lax.rem(to, 2), lax.div(to, 2)

    upper, lower = pl.ds(0, 16), pl.ds(16, 16)
    first = []
    z_copies = []
    for n, (to, d) in enumerate(((2, 3), (6, 5))):
        first.append(
            copy(hb.at[piece(d)], s1.at[n], x_s.at[0, n], x_r.at[0, n], at_z(to))
        )
    for n, (to, rows16) in enumerate(((2, upper), (6, lower))):
        first.append(
            copy(hb.at[(*piece(4), rows16)], s1h.at[n], x_s.at[1, n], x_r.at[1, n], at_z(to))
        )
    for n, (to, rows16) in enumerate(((2, lower), (6, upper))):
        z_copies.append(
            copy(hb.at[(*piece(to), rows16)], r2z.at[n, rows16], x_s.at[2, n], x_r.at[2, n], at_z(to))
        )
    for n, d in enumerate((1, 7)):
        first[n].wait()
        a, b = piece(d)
        m1[n] = (hown[a, b] + s1[n].astype(F32)).astype(BF16)
        z_copies.append(copy(m1.at[n], r1z.at[n], x_s.at[3, n], x_r.at[3, n], at_z(d)))
    for n, (d, rows16) in enumerate(((2, upper), (6, lower))):
        first[2 + n].wait()
        a, b = piece(d)
        m2[n] = (hown[a, b, rows16] + s1h[n].astype(F32)).astype(BF16)
        z_copies.append(
            copy(m2.at[n], r2z.at[n, rows16], x_s.at[4, n], x_r.at[4, n], at_z(d))
        )

    stage_b = []
    for c in stage_a[:3]:
        c.wait()
    total = g2[0, y].astype(F32) + qy[1].astype(F32) + qy[2].astype(F32) + qy[3].astype(F32)
    r0[...] = total
    r0b[...] = total.astype(BF16)
    for d in (2, 1, 3):
        src = r0b.at[lax.rem(x + d, 4)]
        stage_b.append(copy(src, fx.at[d], v_s.at[2, d], v_r.at[2, d], at_x(d)))
    for c in stage_a[3:]:
        c.wait()
    total = g2[1, x].astype(F32) + qx[1].astype(F32) + qx[2].astype(F32) + qx[3].astype(F32)
    r1[...] = total
    r1b[...] = total.astype(BF16)
    for d in (2, 1, 3):
        src = r1b.at[lax.rem(y + d, 4)]
        stage_b.append(copy(src, fy.at[d], v_s.at[3, d], v_r.at[3, d], at_y(d)))
    for c in stage_b:
        c.wait()

    def ordered(v):
        tiles = [v[:, 128 * i:128 * i + 128] for i in range(4)]
        tails = [v[:, 512 + 64 * i:576 + 64 * i] for i in range(4)]
        return jnp.concatenate([t for pair in zip(tiles, tails) for t in pair], axis=1)

    low = r0[x] + fx[1].astype(F32) + fx[2].astype(F32) + fx[3].astype(F32)
    high = r1[y] + fy[1].astype(F32) + fy[2].astype(F32) + fy[3].astype(F32)
    acc = jnp.concatenate([low, high], axis=0)
    held = hcap[...]
    clip_held = hclip[...]
    clip_unit = clip_held.astype(BF16).astype(F32)
    cap_unit = held.astype(BF16).astype(F32)
    pool_unit = pu[home, rows, :]
    grad = acc - 0.5 * clip_unit - 0.5 * pool_unit
    dcap_ref[...] = ordered(
        (grad - held * jnp.sum(held * grad, axis=1, keepdims=True)) / hlen[1]
    )

    for c in z_copies:
        c.wait()
    acc = hown[zl, zh] + r1z[0].astype(F32) + r1z[1].astype(F32)
    acc = acc + r2z[0].astype(F32) + r2z[1].astype(F32)
    grad = acc - 0.5 * cap_unit
    dclip_ref[...] = ordered(
        (grad - clip_held * jnp.sum(clip_held * grad, axis=1, keepdims=True)) / hlen[0]
    )


def body(clips, captions, video_id, logit_scale):
    vmem = pl.BlockSpec(memory_space=pltpu.VMEM)
    hbm = pl.BlockSpec(memory_space=pltpu.HBM)
    dma = lambda *shape: pltpu.SemaphoreType.DMA(shape)
    out = jax.ShapeDtypeStruct((32, 768), F32)
    V = pltpu.VMEM
    keep = lambda v: pltpu.with_memory_space_constraint(v, pltpu.HBM)
    d_clips, d_captions = pl.pallas_call(
        kernel,
        out_shape=(out, out),
        in_specs=[pl.BlockSpec(memory_space=pltpu.SMEM), hbm, hbm, hbm],
        out_specs=(vmem, vmem),
        scratch_shapes=[
            V((2, 192, 128), BF16), V((64, 128), jnp.int32),
            V((4, 48, 128), BF16), V((4, 48, 128), BF16), V((16, 192, 128), BF16),
            V((32, 768), F32), V((32, 768), F32), V((2, 32, 1), F32),
            V((768, 512), BF16), V((2, 4, 4, 16, 768), BF16),
            V((4, 128, 1), F32), V((1, 512), F32), V((1, 512), F32), V((4, 128, 1), F32),
            V((4, 128, 768), F32), V((4, 128, 1), F32), V((4, 1, 768), F32), V((4, 1, 768), F32),
            V((4, 128, 512), F32), V((4, 128, 512), F32), V((512, 512), F32), V((512, 512), F32),
            V((4, 128, 768), F32), V((4, 128), F32),
            V((4, 128), F32), V((16, 4, 128), F32), V((4, 128), F32), V((16, 4, 128), F32),
            V((2, 4, 32, 768), BF16), V((2, 4, 32, 768), BF16), V((2, 4, 32, 768), BF16),
            V((2, 4, 32, 768), F32), V((2, 32, 768), BF16), V((2, 16, 768), BF16),
            V((2, 32, 768), BF16), V((2, 16, 768), BF16), V((2, 32, 768), BF16),
            V((2, 32, 768), BF16),
            V((2, 4, 4, 16, 768), BF16),
            V((4, 4, 16, 768), BF16), V((4, 4, 16, 768), BF16),
            V((4, 16, 768), F32), V((4, 16, 768), F32),
            V((4, 16, 768), BF16), V((4, 16, 768), BF16),
            V((4, 16, 768), BF16), V((4, 16, 768), BF16),
            dma(3), dma(4), dma(4), dma(8), dma(8), dma(8), dma(8), dma(2, 4), dma(2, 4),
            dma(2, 4, 4), dma(2, 4, 4),
            dma(4), dma(4), dma(2, 16), dma(2, 16), dma(1, 2), dma(1, 2), dma(5, 2), dma(5, 2),
            dma(4, 4), dma(4, 4),
        ],
        compiler_params=pltpu.CompilerParams(
            collective_id=0, has_side_effects=True, vmem_limit_bytes=48 * 1024 * 1024
        ),
        name="contrastive",
    )(logit_scale.reshape(1), keep(video_id.reshape(64, 128)), keep(clips.T), keep(captions.T))
    return logit_scale * d_clips, logit_scale * d_captions


def solution(mesh):
    in_specs = (P("dp", "mp"), P("dp", "mp"), P(), P())
    out_specs = (P(("dp", "mp"), None), P(("dp", "mp"), None))
    return jax.shard_map(body, mesh=mesh, in_specs=in_specs, out_specs=out_specs, check_vma=False)
```
